256 devices in a mesh: slab: 2 (over z_lo), freq: 8 (over y, core), energy: 16 (over x, z_hi).
Axes of the slice: x: 4, y: 4, z: 8 (z_hi: 4, z_lo: 2; z = z_hi * 2 + z_lo), core: 2. Of those that a mesh axis runs over, the one named last changes fastest.
Arguments:
- lesser: bfloat16 [32, 4, 2, 512, 512], P('energy', 'slab'), may hold values from -6 to 6
- retarded: bfloat16 [32, 4, 2, 512, 512], P('energy', 'slab'), may hold values from -0.25 to 0.25
- coupling: bfloat16 [16, 512, 512], P('freq'), may hold values from -0.125 to 0.125
- occupations: float32 [16], P('freq'), may hold values from 0.1 to 3
- offsets: int32 [16], P('freq'), may hold values from 1 to 2
- intersection: float32 [4], P('slab'), may hold values from 0.2 to 0.6
Outputs:
- updated: float32 [32, 4, 2, 512, 512], P('energy', 'slab', None, 'freq')
The draws below stay inside these ranges and needn't reach their ends.
All inputs are finite; a program needn't handle non-finite values.
Results may differ from the reference program's by a relative error of at most 0.017.
Values may be sent and summed in bfloat16 or wider, within the bound.
No kernel may reach another device: no remote copies, remote signals or barrier semaphores. Data moves between devices by JAX's collectives and lax.ppermute only.
A program may use at most 128 MiB of HBM per device.

```python
import math
import jax
import jax.numpy as jnp
from jax import lax

NO = 512
OFFMAX = 2
FQ_DEV = 2
ENERGIES = 32
FREQS = 16
SLABS = 4
N_FREQ = 8


def place_ends(drawn, own_key, least, top_value):
    index_at = [jax.random.randint(jax.random.fold_in(own_key, axis), (), 0, length) for axis, length in enumerate(drawn.shape)]
    widest = drawn.shape.index(max(drawn.shape))
    neighbour = index_at[:widest] + [(index_at[widest] + 1) % drawn.shape[widest]] + index_at[widest + 1:]
    return drawn.at[tuple(index_at)].set(least).at[tuple(neighbour)].set(top_value)


def levels(key, shape, cuts, low, top_value):
    def one(dim, shards_of):
        heights = jax.random.uniform(jax.random.fold_in(jax.random.fold_in(key, 6), dim), (shards_of,), jnp.float32, low / len(cuts), top_value / len(cuts))
        return jnp.repeat(jnp.exp(heights), shape[dim] // shards_of).reshape((-1,) + (1,) * (len(shape) - dim - 1))

    factor_of = one(*cuts[0])
    for cut in cuts[1:]:
        factor_of = factor_of * one(*cut)
    return factor_of


def gaussian(own_key, shape, spread, bound, cuts=(), kind=jnp.bfloat16):
    drawn = jax.random.normal(own_key, shape, jnp.float32) * spread
    if len(cuts) > 0:
        drawn = levels(own_key, shape, cuts, -0.22, 0.18) * drawn
    return jnp.clip(drawn, min=-bound, max=bound).astype(kind)


def setup_inputs(seed: int = 0) -> dict:
    splits = jax.random.split(jax.random.key(seed), 7)
    return {
        "lesser": gaussian(splits[0], (ENERGIES, SLABS, 2, NO, NO), 1.0, 6.0, ((0, 16), (1, 2))),
        "retarded": gaussian(splits[1], (ENERGIES, SLABS, 2, NO, NO), NO ** -0.5, 0.25, ((0, 16), (1, 2))),
        "coupling": gaussian(splits[2], (FREQS, NO, NO), (4 * NO) ** -0.5, 0.125, ((0, 8),)),
        "occupations": jnp.clip(jnp.exp(math.log(3.0) - 3.4011974 * jax.random.uniform(splits[3], (FREQS,), jnp.float32) ** levels(splits[3], (FREQS,), ((0, 8),), -0.2, 0.2)), 0.1, 3.0),
        "offsets": place_ends(jax.random.randint(splits[4], (FREQS,), 1, OFFMAX + 1), jax.random.fold_in(splits[4], 1), 1, OFFMAX).astype(jnp.int32),
        "intersection": jnp.clip(0.2 + 0.400000021 * jax.random.uniform(splits[5], (SLABS,), jnp.float32) ** levels(splits[5], (SLABS,), ((0, 2),), -0.2, 0.2), 0.2, 0.6),
    }


def reference(lesser, retarded, coupling, occupations, offsets, intersection):
    padded = jnp.pad(lesser, ((OFFMAX, OFFMAX), (0, 0), (0, 0), (0, 0), (0, 0)))
    group_coupling = coupling.reshape(N_FREQ, FQ_DEV, NO, NO)
    group_numbers = occupations.reshape(N_FREQ, FQ_DEV)
    group_shifts = offsets.reshape(N_FREQ, FQ_DEV)

    def energy_term(energy_index):
        def group_add(accumulated, group):
            weights, numbers, shifts = group
            lower_index = (energy_index + OFFMAX - shifts).astype(jnp.int32)
            upper_index = (energy_index + OFFMAX + shifts).astype(jnp.int32)
            lower_green = jnp.take(padded, lower_index, axis=0).astype(jnp.float32)
            upper_green = jnp.take(padded, upper_index, axis=0).astype(jnp.float32)
            scale = numbers[:, None, None, None, None]
            mixture = scale * lower_green + (scale + 1.0) * upper_green
            mixture = lax.optimization_barrier(mixture.astype(jnp.bfloat16)).astype(jnp.float32)
            weights_wide = weights.astype(jnp.float32)
            left_product = jnp.einsum('fij,fscjk->fscik', weights_wide, mixture)
            left_product = lax.optimization_barrier(left_product.astype(jnp.bfloat16)).astype(jnp.float32)
            sandwich = jnp.einsum('fscik,fmk->scim', left_product, weights_wide)
            rounded = lax.optimization_barrier(sandwich.astype(jnp.bfloat16)).astype(jnp.float32)
            return accumulated + rounded, None

        initial = jnp.zeros((SLABS, 2, NO, NO), jnp.float32)
        result, unused = lax.scan(group_add, initial, (group_coupling, group_numbers, group_shifts))
        return result

    self_energy = lax.map(energy_term, jnp.arange(ENERGIES, dtype=jnp.int32))
    self_half = lax.optimization_barrier(self_energy.astype(jnp.bfloat16)).astype(jnp.float32)
    beside = jnp.pad(self_half, ((0, 0), (1, 1), (0, 0), (0, 0), (0, 0)))
    combined = self_half + intersection[None, :, None, None, None] * (beside[:, :-2] + beside[:, 2:])
    combined = lax.optimization_barrier(combined.astype(jnp.bfloat16)).astype(jnp.float32)
    green = retarded.astype(jnp.float32)
    real_green = green[:, :, 0]
    imag_green = green[:, :, 1]
    real_self = combined[:, :, 0]
    imag_self = combined[:, :, 1]

    def by_transpose(left_side, right_side):
        return jnp.einsum('esij,eskj->esik', left_side, right_side)

    real_part = by_transpose(real_self, real_green) + by_transpose(imag_self, imag_green)
    imag_part = by_transpose(imag_self, real_green) - by_transpose(real_self, imag_green)
    product = jnp.stack([real_part, imag_part], axis=2)
    product = lax.optimization_barrier(product.astype(jnp.bfloat16)).astype(jnp.float32)
    real_product = product[:, :, 0]
    imag_product = product[:, :, 1]

    def plain_product(left_side, right_side):
        return jnp.einsum('esij,esjk->esik', left_side, right_side)

    out_real = plain_product(real_green, real_product) - plain_product(imag_green, imag_product)
    out_imag = plain_product(real_green, imag_product) + plain_product(imag_green, real_product)
    return jnp.stack([out_real, out_imag], axis=2)
```

```python
import functools
import jax
import jax.numpy as jnp
from jax import lax
from jax.experimental import pallas as pl
from jax.experimental.pallas import tpu as pltpu
from jax.sharding import PartitionSpec as P

NO = 512
ROWS = 64
F32 = jnp.float32
BF16 = jnp.bfloat16
MIB = 1 << 20


def any_spec():
    return pl.BlockSpec(memory_space=pl.ANY)


def smem_spec():
    return pl.BlockSpec(memory_space=pltpu.SMEM)


def vmem_spec():
    return pl.BlockSpec(memory_space=pltpu.VMEM)


def mul(a, b):
    return jnp.dot(a, b, preferred_element_type=F32)


def mul_t(a, b):
    return lax.dot_general(a, b, (((1,), (1,)), ((), ())), preferred_element_type=F32)


def sandwich_kernel(owners, first, last, place, table, lesser, g1, g2, g3, *rest):
    arrays = rest[: len(owners)]
    rest = rest[len(owners):]
    if not first:
        start, rest = rest[0], rest[1:]
    out, green, coup, acc, gsem, csem, asem = rest
    y, k, i, sl = place[0], place[1], place[2], place[3]
    copies = []
    for n, src in enumerate((lesser.at[1 - i, sl, k], g1, g2, g3)):
        copies.append(pltpu.make_async_copy(src, green.at[n], gsem.at[n]))
    for c in copies:
        c.start()
    moves, where = [], []
    for ref, (dy, dk, f0, count) in zip(arrays, owners):
        for t in range(count):
            n = len(moves)
            moves.append(pltpu.make_async_copy(ref.at[t], coup.at[n], csem.at[n]))
            moves[-1].start()
            where.append(2 * (2 * (y ^ dy) + (k ^ dk)) + f0 + t)
    if not first:
        begin = pltpu.make_async_copy(start, acc, asem.at[0])
        begin.start()
    for c in copies:
        c.wait()
    if not first:
        begin.wait()
    for n, f in enumerate(where):
        scale = table[0, f]
        far = table[1, f] > 1.5
        low = jnp.where(i == 0, jnp.where(far, 3, 1), jnp.where(far, 1, 0))
        high = jnp.where(i == 0, jnp.where(far, 2, 0), jnp.where(far, 3, 2))
        mixture = (
            scale * green[low].astype(F32) + (scale + 1.0) * green[high].astype(F32)
        ).astype(BF16)
        moves[n].wait()
        left = mul(coup[n], mixture).astype(BF16)
        term = mul_t(left, coup[n])
        if n == 0 and first:
            acc[...] = term
        elif n == len(where) - 1:
            out[...] = (acc[...] + term).astype(out.dtype)
        else:
            acc[...] += term


def sandwich(owners, place, table, lesser, greens, arrays, start, last):
    count = sum(o[3] for o in owners)
    first = start is None
    operands = [place, table, lesser, *greens, *arrays] + ([] if first else [start])
    flops = count * 4 * NO**3
    return pl.pallas_call(
        functools.partial(sandwich_kernel, owners, first, last),
        out_shape=jax.ShapeDtypeStruct((NO, NO), BF16 if last else F32),
        in_specs=[smem_spec(), smem_spec()] + [any_spec()] * (len(operands) - 2),
        out_specs=vmem_spec(),
        scratch_shapes=[
            pltpu.VMEM((4, NO, NO), BF16),
            pltpu.VMEM((count, NO, NO), BF16),
            pltpu.VMEM((NO, NO), F32),
            pltpu.SemaphoreType.DMA((4,)),
            pltpu.SemaphoreType.DMA((count,)),
            pltpu.SemaphoreType.DMA((1,)),
        ],
        compiler_params=pltpu.CompilerParams(vmem_limit_bytes=40 * MIB),
        cost_estimate=pl.CostEstimate(
            flops=flops, bytes_accessed=(count + 8) * NO * NO * 2, transcendentals=0
        ),
        name="sandwich_last" if last else "sandwich_first",
    )(*operands)


def update_kernel(place, own_c, other_c, retarded, own_out, out1, out2, out3, green, sem):
    y, k, i, sl = place[0], place[1], place[2], place[3]
    copy = pltpu.make_async_copy(retarded.at[i, sl], green, sem.at[0])
    copy.start()
    copy.wait()
    a, b = green[0], green[1]
    mine, other = own_c[...], other_c[...]
    real = jnp.where(k == 0, mine, other)
    imag = jnp.where(k == 0, other, mine)
    yr = (mul_t(real, a) + mul_t(imag, b)).astype(BF16)
    yi = (mul_t(imag, a) - mul_t(real, b)).astype(BF16)
    for dy, ref in ((0, own_out), (1, out1), (2, out2), (3, out3)):
        first = pl.multiple_of((2 * (y ^ dy) + k) * ROWS, ROWS)
        ar = green[0, pl.ds(first, ROWS), :]
        br = green[1, pl.ds(first, ROWS), :]
        ref[0] = (mul(ar, yr) - mul(br, yi)).astype(ref.dtype)
        ref[1] = (mul(ar, yi) + mul(br, yr)).astype(ref.dtype)


def update(place, own_c, other_c, retarded):
    piece = (2, ROWS, NO)
    return pl.pallas_call(
        update_kernel,
        out_shape=[jax.ShapeDtypeStruct(piece, F32)] + [jax.ShapeDtypeStruct(piece, BF16)] * 3,
        in_specs=[smem_spec(), vmem_spec(), vmem_spec(), any_spec()],
        out_specs=[vmem_spec()] * 4,
        scratch_shapes=[pltpu.VMEM((2, NO, NO), BF16), pltpu.SemaphoreType.DMA((1,))],
        compiler_params=pltpu.CompilerParams(vmem_limit_bytes=40 * MIB),
        cost_estimate=pl.CostEstimate(
            flops=12 * NO**3, bytes_accessed=5 * NO * NO * 2, transcendentals=0
        ),
        name="update",
    )(place, own_c, other_c, retarded)


def collect_kernel(place, own, p1, p2, p3, out):
    y, b = place[0], place[4]
    for dy, ref in ((0, own), (1, p1), (2, p2), (3, p3)):
        source = y ^ dy
        out[source // 2, (source % 2) ^ b] = ref[...].astype(F32)


def collect(place, pieces):
    return pl.pallas_call(
        collect_kernel,
        out_shape=jax.ShapeDtypeStruct((2, 2, 2, ROWS, NO), F32),
        in_specs=[smem_spec()] + [vmem_spec()] * 4,
        out_specs=vmem_spec(),
        compiler_params=pltpu.CompilerParams(vmem_limit_bytes=40 * MIB),
        name="collect",
    )(place, *pieces)


def shards(lesser, retarded, coupling, occupations, offsets, intersection):
    fr = lax.axis_index("freq")
    b = lax.axis_index("slab")
    y, k = fr // 2, fr % 2
    i, sl = y // 2, (y % 2) ^ b
    place = jnp.stack([y, k, i, sl, b]).astype(jnp.int32)

    def chip(x, dy):
        return lax.ppermute(x, "freq", [(d, d ^ (2 * dy)) for d in range(8)])

    def core(x):
        return lax.ppermute(x, "freq", [(d, d ^ 1) for d in range(8)])

    count = lax.axis_size("energy")
    up = [(e, e + 1) for e in range(count - 1)]
    down = [(t, s) for s, t in up]
    third = [
        (d * count + s, d * count + t) for d in range(8) for s, t in (up if d < 4 else down)
    ]
    g1 = lax.ppermute(lesser[1, sl, k], "energy", up)
    g2 = lax.ppermute(lesser[0, sl, k], "energy", down)
    g3 = lax.ppermute(lesser[i, sl, k], ("freq", "energy"), third)
    greens = (g1, g2, g3)
    table = jnp.stack([occupations, offsets.astype(F32)], axis=1)
    table = lax.all_gather(table, "freq", axis=0, tiled=True).T

    c1, c3 = chip(coupling, 1), chip(coupling, 3)
    q0 = chip(c3[0:1], 1)
    q1 = chip(c1[1:2], 3)
    s0, s1, s3 = core(coupling), core(c1), core(c3)
    r0, r1 = core(q0), core(q1)

    part = sandwich(
        [(0, 0, 0, 2), (0, 1, 0, 2), (1, 0, 0, 2), (3, 0, 0, 2), (1, 1, 0, 2), (3, 1, 0, 2)],
        place, table, lesser, greens, [coupling, s0, c1, c3, s1, s3], None, False,
    )
    own = sandwich(
        [(2, 0, 0, 1), (2, 0, 1, 1), (2, 1, 0, 1), (2, 1, 1, 1)],
        place, table, lesser, greens, [q0, q1, r0, r1], part, True,
    )
    inner = chip(own, 1)
    edge = [(s * 8 + d, (1 - s) * 8 + d) for s in range(2) for d in range(8) if (d // 2) % 2]
    outer = lax.ppermute(own, ("slab", "freq"), edge)
    combined = (
        own.astype(F32) + intersection[sl] * (inner.astype(F32) + outer.astype(F32))
    ).astype(BF16)
    mine, o1, o2, o3 = update(place, combined, core(combined), retarded)
    return collect(place, (mine, chip(o1, 1), chip(o2, 2), chip(o3, 3)))


def solution(mesh):
    return jax.shard_map(
        shards,
        mesh=mesh,
        in_specs=(
            P("energy", "slab", None, None, None),
            P("energy", "slab", None, None, None),
            P("freq", None, None),
            P("freq"),
            P("freq"),
            P("slab"),
        ),
        out_specs=P("energy", "slab", None, "freq", None),
        check_vma=False,
    )
```

```python
import functools
import jax
import jax.numpy as jnp
from jax import lax
from jax.experimental import pallas as pl
from jax.experimental.pallas import tpu as pltpu
from jax.sharding import PartitionSpec as P

NO = 512
ROWS = 64
F32 = jnp.float32
BF16 = jnp.bfloat16
MIB = 1 << 20


def hbm_spec():
    return pl.BlockSpec(memory_space=pltpu.HBM)


def smem_spec():
    return pl.BlockSpec(memory_space=pltpu.SMEM)


def vmem_spec():
    return pl.BlockSpec(memory_space=pltpu.VMEM)


def mul(a, b):
    return jnp.dot(a, b, preferred_element_type=F32)


def mul_t(a, b):
    return lax.dot_general(a, b, (((1,), (1,)), ((), ())), preferred_element_type=F32)


def sandwich_kernel(owners, first, last, place, table, own, g1, g2, g3, *rest):
    arrays = rest[: len(owners)]
    rest = rest[len(owners):]
    if first:
        home, rest = rest[0], rest[1:]
    else:
        start, rest = rest[0], rest[1:]
    out, green, acc, gsem, *rest = rest
    y, k, i = place[0], place[1], place[2]
    copies = [
        pltpu.make_async_copy(src, green.at[n], gsem.at[n])
        for n, src in enumerate((own, g1, g2, g3))
    ]
    for c in copies:
        c.start()
    todo = []
    for ref, (dy, dk, f0, count) in zip(arrays, owners):
        for t in range(count):
            todo.append((ref, t, 2 * (2 * (y ^ dy) + (k ^ dk)) + f0 + t, None))
    if first:
        coup, csem = rest
        move = pltpu.make_async_copy(home, coup, csem.at[0])
        move.start()
        for t in range(2):
            todo.append((coup, t, 2 * (2 * y + k) + t, move if t == 0 else None))
    for c in copies:
        c.wait()
    for n, (ref, t, f, move) in enumerate(todo):
        scale = table[0, f]
        far = table[1, f] > 1.5
        low = jnp.where(i == 0, jnp.where(far, 3, 1), jnp.where(far, 1, 0))
        high = jnp.where(i == 0, jnp.where(far, 2, 0), jnp.where(far, 3, 2))
        mixture = (
            scale * green[low].astype(F32) + (scale + 1.0) * green[high].astype(F32)
        ).astype(BF16)
        if move is not None:
            move.wait()
        left = mul(ref[t], mixture).astype(BF16)
        term = mul_t(left, ref[t])
        so_far = (None if first else start[...]) if n == 0 else acc[...]
        total = term if so_far is None else so_far + term
        if n == len(todo) - 1:
            out[...] = total.astype(out.dtype)
        else:
            acc[...] = total


def sandwich(owners, place, table, greens, arrays, home, start, last):
    first = start is None
    count = sum(o[3] for o in owners) + (2 if first else 0)
    operands = [place, table, *greens, *arrays, home if first else start]
    scratch = [
        pltpu.VMEM((4, NO, NO), BF16),
        pltpu.VMEM((NO, NO), F32),
        pltpu.SemaphoreType.DMA((4,)),
    ]
    if first:
        scratch += [pltpu.VMEM((2, NO, NO), BF16), pltpu.SemaphoreType.DMA((1,))]
    return pl.pallas_call(
        functools.partial(sandwich_kernel, owners, first, last),
        out_shape=jax.ShapeDtypeStruct((NO, NO), BF16 if last else F32),
        in_specs=[smem_spec(), smem_spec()]
        + [vmem_spec()] * (len(operands) - 3)
        + [hbm_spec() if first else vmem_spec()],
        out_specs=vmem_spec(),
        scratch_shapes=scratch,
        compiler_params=pltpu.CompilerParams(vmem_limit_bytes=24 * MIB),
        cost_estimate=pl.CostEstimate(
            flops=count * 4 * NO**3, bytes_accessed=(count + 8) * NO * NO * 2, transcendentals=0
        ),
        name="sandwich_last" if last else "sandwich_first",
    )(*operands)


def update_kernel(place, own_c, other_c, green, own_out, out1, out2, out3):
    y, k = place[0], place[1]
    a, b = green[0], green[1]
    mine, other = own_c[...], other_c[...]
    real = jnp.where(k == 0, mine, other)
    imag = jnp.where(k == 0, other, mine)
    yr = (mul_t(real, a) + mul_t(imag, b)).astype(BF16)
    yi = (mul_t(imag, a) - mul_t(real, b)).astype(BF16)
    for dy, ref in ((0, own_out), (1, out1), (2, out2), (3, out3)):
        first = pl.multiple_of((2 * (y ^ dy) + k) * ROWS, ROWS)
        ar = green[0, pl.ds(first, ROWS), :]
        br = green[1, pl.ds(first, ROWS), :]
        ref[0] = (mul(ar, yr) - mul(br, yi)).astype(ref.dtype)
        ref[1] = (mul(ar, yi) + mul(br, yr)).astype(ref.dtype)


def update(place, own_c, other_c, retarded):
    piece = (2, ROWS, NO)
    return pl.pallas_call(
        update_kernel,
        out_shape=[jax.ShapeDtypeStruct(piece, F32)] + [jax.ShapeDtypeStruct(piece, BF16)] * 3,
        in_specs=[smem_spec(), vmem_spec(), vmem_spec(), vmem_spec()],
        out_specs=[vmem_spec()] * 4,
        compiler_params=pltpu.CompilerParams(vmem_limit_bytes=24 * MIB),
        cost_estimate=pl.CostEstimate(
            flops=12 * NO**3, bytes_accessed=5 * NO * NO * 2, transcendentals=0
        ),
        name="update",
    )(place, own_c, other_c, retarded)


def collect_kernel(place, own, p1, p2, p3, out):
    y, b = place[0], place[4]
    for dy, ref in ((0, own), (1, p1), (2, p2), (3, p3)):
        source = y ^ dy
        out[source // 2, (source % 2) ^ b] = ref[...].astype(F32)


def collect(place, pieces):
    return pl.pallas_call(
        collect_kernel,
        out_shape=jax.ShapeDtypeStruct((2, 2, 2, ROWS, NO), F32),
        in_specs=[smem_spec()] + [vmem_spec()] * 4,
        out_specs=vmem_spec(),
        compiler_params=pltpu.CompilerParams(vmem_limit_bytes=24 * MIB),
        name="collect",
    )(place, *pieces)


def shards(lesser, retarded, coupling, occupations, offsets, intersection):
    fr = lax.axis_index("freq")
    b = lax.axis_index("slab")
    y, k = fr // 2, fr % 2
    i, sl = y // 2, (y % 2) ^ b
    place = jnp.stack([y, k, i, sl, b]).astype(jnp.int32)

    def chip(x, dy):
        return lax.ppermute(x, "freq", [(d, d ^ (2 * dy)) for d in range(8)])

    def core(x):
        return lax.ppermute(x, "freq", [(d, d ^ 1) for d in range(8)])

    count = lax.axis_size("energy")
    up = [(e, e + 1) for e in range(count - 1)]
    down = [(t, s) for s, t in up]
    third = [
        (d * count + s, d * count + t) for d in range(8) for s, t in (up if d < 4 else down)
    ]
    g1 = lax.ppermute(lesser[1, sl, k], "energy", up)
    g2 = lax.ppermute(lesser[0, sl, k], "energy", down)
    g3 = lax.ppermute(lesser[i, sl, k], ("freq", "energy"), third)
    greens = (lesser[1 - i, sl, k], g1, g2, g3)
    table = jnp.stack([occupations, offsets.astype(F32)], axis=1)
    table = lax.all_gather(table, "freq", axis=0, tiled=True).T

    c1, c3, s0 = chip(coupling, 1), chip(coupling, 3), core(coupling)
    c1, c3, table, green = lax.optimization_barrier((c1, c3, table, retarded[i, sl]))
    q0 = chip(c3[0:1], 1)
    q1 = chip(c1[1:2], 3)
    c1, c3, q0, q1 = lax.optimization_barrier((c1, c3, q0, q1))
    s1, s3, r0, r1 = core(c1), core(c3), core(q0), core(q1)

    part = sandwich(
        [(1, 0, 0, 2), (3, 0, 0, 2), (2, 0, 0, 1), (2, 0, 1, 1)],
        place, table, greens, [c1, c3, q0, q1], coupling, None, False,
    )
    own = sandwich(
        [(0, 1, 0, 2), (1, 1, 0, 2), (3, 1, 0, 2), (2, 1, 0, 1), (2, 1, 1, 1)],
        place, table, greens, [s0, s1, s3, r0, r1], None, part, True,
    )
    inner = chip(own, 1)
    edge = [(s * 8 + d, (1 - s) * 8 + d) for s in range(2) for d in range(8) if (d // 2) % 2]
    outer = lax.ppermute(own, ("slab", "freq"), edge)
    combined = (
        own.astype(F32) + intersection[sl] * (inner.astype(F32) + outer.astype(F32))
    ).astype(BF16)
    mine, o1, o2, o3 = update(place, combined, core(combined), green)
    return collect(place, (mine, chip(o1, 1), chip(o2, 2), chip(o3, 3)))


def solution(mesh):
    return jax.shard_map(
        shards,
        mesh=mesh,
        in_specs=(
            P("energy", "slab", None, None, None),
            P("energy", "slab", None, None, None),
            P("freq", None, None),
            P("freq"),
            P("freq"),
            P("slab"),
        ),
        out_specs=P("energy", "slab", None, "freq", None),
        check_vma=False,
    )
```

```python
import functools
import jax
import jax.numpy as jnp
from jax import lax
from jax.experimental import pallas as pl
from jax.experimental.pallas import tpu as pltpu
from jax.sharding import PartitionSpec as P

NO = 512
ROWS = 64
TAIL = 16
F32 = jnp.float32
BF16 = jnp.bfloat16
MIB = 1 << 20
HBM = pl.BlockSpec(memory_space=pltpu.HBM)
SMEM = pl.BlockSpec(memory_space=pltpu.SMEM)
VMEM = pl.BlockSpec(memory_space=pltpu.VMEM)
PARAMS = pltpu.CompilerParams(vmem_limit_bytes=24 * MIB)


def shape(dims, kind):
    return jax.ShapeDtypeStruct(dims, kind)


def mul(a, b):
    return jnp.dot(a, b, preferred_element_type=F32)


def mul_t(a, b):
    return lax.dot_general(a, b, (((1,), (1,)), ((), ())), preferred_element_type=F32)


def prepare_kernel(place, occupations, offsets, coupling, lesser, packed, near, far, tail, sem):
    k, sl, c = place[1], place[2], place[4]
    copies = [
        pltpu.make_async_copy(lesser.at[1 - k, sl, c], near, sem.at[0]),
        pltpu.make_async_copy(lesser.at[k, sl, c], far, sem.at[1]),
    ]
    for t in range(2):
        copies.append(
            pltpu.make_async_copy(coupling.at[t], packed.at[t, pl.ds(0, NO)], sem.at[2 + t])
        )
    for copy in copies:
        copy.start()
    row = lax.broadcasted_iota(jnp.int32, (TAIL, NO), 0)
    for t in range(2):
        whole = jnp.full((TAIL, NO), occupations[t], F32)
        high = whole.astype(BF16).astype(F32)
        middle = (whole - high).astype(BF16).astype(F32)
        low = whole - high - middle
        steps = jnp.full((TAIL, NO), offsets[t], jnp.int32).astype(F32)
        rows = jnp.where(row == 0, high, jnp.where(row == 1, middle, jnp.where(row == 2, low, steps)))
        tail[t] = rows.astype(BF16)
        copies.append(
            pltpu.make_async_copy(tail.at[t], packed.at[t, pl.ds(NO, TAIL)], sem.at[4 + t])
        )
        copies[-1].start()
    for copy in copies:
        copy.wait()


def prepare(place, occupations, offsets, coupling, lesser):
    return pl.pallas_call(
        prepare_kernel,
        out_shape=[shape((2, NO + TAIL, NO), BF16)] + [shape((NO, NO), BF16)] * 2,
        in_specs=[SMEM] * 3 + [HBM] * 2,
        out_specs=[HBM] * 3,
        scratch_shapes=[pltpu.VMEM((2, TAIL, NO), BF16), pltpu.SemaphoreType.DMA((6,))],
        compiler_params=pltpu.CompilerParams(vmem_limit_bytes=60 * MIB),
        name="prepare",
    )(place, occupations, offsets, coupling, lesser)


def add_terms(k, green, todo, coup, csem, begin):
    def copy_of(n):
        return pltpu.make_async_copy(todo[n], coup.at[n], csem.at[n])

    def arrive(n):
        copy_of(n).wait()
        tail = coup[n, NO:, :].astype(F32)
        scale = tail[0:1] + tail[1:2] + tail[2:3]
        return scale, (jnp.max(tail[3:4, 0:128]) > 1.5).astype(jnp.int32)

    for n in range(min(3, len(todo))):
        copy_of(n).start()
    begin()
    numbers = arrive(0)
    for n in range(len(todo)):
        scale, far = numbers
        if n + 3 < len(todo):
            copy_of(n + 3).start()
        if n + 1 < len(todo):
            numbers = arrive(n + 1)
        low = (1 - k) + 2 * far
        high = k + 2 * far
        mixture = (
            scale * green[low].astype(F32) + (scale + 1.0) * green[high].astype(F32)
        ).astype(BF16)
        weights = coup[n, :NO, :]
        left = mul(weights, mixture).astype(BF16)
        yield mul_t(left, weights)


def first_kernel(place, own, near, shared, far, home, s0, c1, c3, out, green, coup, gsem, csem):
    k = place[1]
    copies = [
        pltpu.make_async_copy(src, green.at[n], gsem.at[n])
        for n, src in enumerate((own, near, shared, far))
    ]
    for copy in copies:
        copy.start()

    def begin():
        for copy in copies:
            copy.wait()

    todo = [ref.at[t] for ref in (home, s0, c1, c3) for t in range(2)]
    for n, term in enumerate(add_terms(k, green, todo, coup, csem, begin)):
        out[...] = term if n == 0 else out[...] + term


def last_kernel(
    place, green, start, s1, s3, c2, s2, retarded,
    out, whole, blocks, coup, acc, csem, rsem,
):
    y, k, sl = place[0], place[1], place[2]
    copies = [pltpu.make_async_copy(retarded.at[k, sl], whole, rsem.at[0])]
    for dest in range(8):
        target = 2 * y + k ^ dest
        first = pl.multiple_of(target * ROWS, ROWS)
        copies.append(
            pltpu.make_async_copy(
                retarded.at[k, sl, :, pl.ds(first, ROWS)],
                blocks.at[:, pl.ds(dest * ROWS, ROWS)],
                rsem.at[1 + dest],
            )
        )
    todo = [ref.at[t] for ref in (s1, s3, c2, s2) for t in range(2)]

    def begin():
        for copy in copies:
            copy.start()

    for n, term in enumerate(add_terms(k, green, todo, coup, csem, begin)):
        total = (start if n == 0 else acc)[...] + term
        if n == len(todo) - 1:
            out[...] = total.astype(BF16)
        else:
            acc[...] = total
    for copy in copies:
        copy.wait()


def sandwich_first(place, own, near, shared, far, arrays):
    return pl.pallas_call(
        first_kernel,
        out_shape=[shape((NO, NO), F32), shape((4, NO, NO), BF16)],
        in_specs=[SMEM] + [HBM] * 8,
        out_specs=[VMEM] * 2,
        scratch_shapes=[
            pltpu.VMEM((8, NO + TAIL, NO), BF16),
            pltpu.SemaphoreType.DMA((4,)),
            pltpu.SemaphoreType.DMA((8,)),
        ],
        compiler_params=PARAMS,
        cost_estimate=pl.CostEstimate(
            flops=8 * 4 * NO**3, bytes_accessed=18 * NO * NO * 2, transcendentals=0
        ),
        name="sandwich_first",
    )(place, own, near, shared, far, *arrays)


def sandwich_last(place, green, start, arrays, retarded):
    return pl.pallas_call(
        last_kernel,
        out_shape=[shape((NO, NO), BF16), shape((2, NO, NO), BF16), shape((2, NO, NO), BF16)],
        in_specs=[SMEM] + [VMEM] * 2 + [HBM] * 5,
        out_specs=[VMEM] * 3,
        scratch_shapes=[
            pltpu.VMEM((8, NO + TAIL, NO), BF16),
            pltpu.VMEM((NO, NO), F32),
            pltpu.SemaphoreType.DMA((8,)),
            pltpu.SemaphoreType.DMA((9,)),
        ],
        compiler_params=PARAMS,
        cost_estimate=pl.CostEstimate(
            flops=8 * 4 * NO**3, bytes_accessed=18 * NO * NO * 2, transcendentals=0
        ),
        name="sandwich_last",
    )(place, green, start, *arrays, retarded)


def update_kernel(place, weight, own, inner, outer, whole, blocks, *outs):
    sl, c = place[2], place[4]
    beside = inner[...].astype(F32) + outer[...].astype(F32)
    combined = (own[...].astype(F32) + weight[sl] * beside).astype(BF16)
    a_side = mul_t(combined, whole[0]).astype(BF16)
    b_side = mul_t(combined, whole[1]).astype(BF16)
    a, b = blocks[0], blocks[1]
    real = mul(a, a_side) + mul(b, b_side)
    imag = mul(b, a_side) - mul(a, b_side)
    first = jnp.where(c == 0, real, -imag)
    second = jnp.where(c == 0, imag, real)
    for dest, ref in enumerate(outs):
        rows = slice(dest * ROWS, (dest + 1) * ROWS)
        ref[0] = first[rows].astype(ref.dtype)
        ref[1] = second[rows].astype(ref.dtype)


def update(place, weight, own, inner, outer, whole, blocks):
    piece = (2, ROWS, NO)
    return pl.pallas_call(
        update_kernel,
        out_shape=[shape(piece, F32)] + [shape(piece, BF16)] * 7,
        in_specs=[SMEM] * 2 + [VMEM] * 5,
        out_specs=[VMEM] * 8,
        compiler_params=PARAMS,
        cost_estimate=pl.CostEstimate(
            flops=12 * NO**3, bytes_accessed=10 * NO * NO * 2, transcendentals=0
        ),
        name="update",
    )(place, weight, own, inner, outer, whole, blocks)


def collect_kernel(place, *refs):
    *pieces, out = refs
    y, k, b = place[0], place[1], place[3]
    for dk in range(2):
        for dp in range(2):
            total = pieces[2 * dp + dk][...].astype(F32) + pieces[2 * (dp + 2) + dk][...].astype(F32)
            out[k ^ dk, ((y ^ dp) & 1) ^ b] = total


def collect(place, pieces):
    return pl.pallas_call(
        collect_kernel,
        out_shape=shape((2, 2, 2, ROWS, NO), F32),
        in_specs=[SMEM] + [VMEM] * 8,
        out_specs=VMEM,
        compiler_params=PARAMS,
        name="collect",
    )(place, *pieces)


def shards(lesser, retarded, coupling, occupations, offsets, intersection):
    fr = lax.axis_index("freq")
    b = lax.axis_index("slab")
    y, k = fr >> 1, fr & 1
    place = jnp.stack([y, k, (y & 1) ^ b, b, y >> 1]).astype(jnp.int32)

    def flip(x, bits):
        return lax.ppermute(x, "freq", [(d, d ^ bits) for d in range(8)])

    count = lax.axis_size("energy")
    across = []
    for d in range(8):
        for e in range(count):
            target = e + 1 if d % 2 == 0 else e - 1
            if 0 <= target < count:
                across.append((d * count + e, d * count + target))

    packed, own, mine = prepare(place, occupations, offsets, coupling, lesser)
    c2, c1, c3 = flip(packed, 4), flip(packed, 2), flip(packed, 6)
    near = lax.ppermute(own, ("freq", "energy"), across)
    far = lax.ppermute(mine, ("freq", "energy"), across)
    s0 = flip(packed, 1)
    shared, s1, s3, s2 = flip(near, 1), flip(c1, 1), flip(c3, 1), flip(c2, 1)

    part, green = sandwich_first(place, own, near, shared, far, [packed, s0, c1, c3])
    total, whole, blocks = sandwich_last(place, green, part, [s1, s3, c2, s2], retarded)
    inner = flip(total, 2)
    edge = [(s * 8 + d, (1 - s) * 8 + d) for s in range(2) for d in range(8) if (d // 2) % 2]
    outer = lax.ppermute(total, ("slab", "freq"), edge)
    pieces = update(place, intersection, total, inner, outer, whole, blocks)
    return collect(place, [pieces[0]] + [flip(pieces[n], n) for n in range(1, 8)])


def solution(mesh):
    return jax.shard_map(
        shards,
        mesh=mesh,
        in_specs=(
            P("energy", "slab", None, None, None),
            P("energy", "slab", None, None, None),
            P("freq", None, None),
            P("freq"),
            P("freq"),
            P("slab"),
        ),
        out_specs=P("energy", "slab", None, "freq", None),
        check_vma=False,
    )
```

```python
import functools
import jax
import jax.numpy as jnp
from jax import lax
from jax.experimental import pallas as pl
from jax.experimental.pallas import tpu as pltpu
from jax.sharding import PartitionSpec as P

NO = 512
ROWS = 64
TAIL = 16
F32 = jnp.float32
BF16 = jnp.bfloat16
MIB = 1 << 20
HBM = pl.BlockSpec(memory_space=pltpu.HBM)
SMEM = pl.BlockSpec(memory_space=pltpu.SMEM)
VMEM = pl.BlockSpec(memory_space=pltpu.VMEM)
PARAMS = pltpu.CompilerParams(vmem_limit_bytes=24 * MIB)


def shape(dims, kind):
    return jax.ShapeDtypeStruct(dims, kind)


def mul(a, b):
    return jnp.dot(a, b, preferred_element_type=F32)


def mul_t(a, b):
    return lax.dot_general(a, b, (((1,), (1,)), ((), ())), preferred_element_type=F32)


def prepare_kernel(
    place, occupations, offsets, coupling, lesser, packed, half, near, far, sem
):
    k, sl, c, x = place[1], place[2], place[4], place[5]
    copies = [
        pltpu.make_async_copy(lesser.at[1 - k, sl, c], near, sem.at[0]),
        pltpu.make_async_copy(lesser.at[k, sl, c], far, sem.at[1]),
        pltpu.make_async_copy(coupling.at[x], half.at[pl.ds(0, NO)], sem.at[2]),
    ]
    for t in range(2):
        copies.append(
            pltpu.make_async_copy(coupling.at[t], packed.at[t, pl.ds(0, NO)], sem.at[3 + t])
        )
    for copy in copies:
        copy.start()
    row = lax.broadcasted_iota(jnp.int32, (TAIL, NO), 0)

    def tail_of(t):
        whole = jnp.full((TAIL, NO), occupations[t], F32)
        high = whole.astype(BF16).astype(F32)
        middle = (whole - high).astype(BF16).astype(F32)
        low = whole - high - middle
        steps = jnp.full((TAIL, NO), offsets[t], jnp.int32).astype(F32)
        rows = jnp.where(row == 2, low, steps)
        return jnp.where(row == 0, high, jnp.where(row == 1, middle, rows)).astype(BF16)

    packed[0, NO:] = tail_of(0)
    packed[1, NO:] = tail_of(1)
    half[NO:] = tail_of(x)
    for copy in copies:
        copy.wait()


def prepare(place, occupations, offsets, coupling, lesser):
    block = (NO + TAIL, NO)
    return pl.pallas_call(
        prepare_kernel,
        out_shape=[shape((2, *block), BF16), shape(block, BF16)] + [shape((NO, NO), BF16)] * 2,
        in_specs=[SMEM] * 3 + [HBM] * 2,
        out_specs=[VMEM] * 4,
        scratch_shapes=[pltpu.SemaphoreType.DMA((5,))],
        compiler_params=pltpu.CompilerParams(vmem_limit_bytes=60 * MIB),
        name="prepare",
    )(place, occupations, offsets, coupling, lesser)


def add_terms(k, green, todo):
    def numbers_of(block):
        tail = block[NO:, :].astype(F32)
        scale = tail[0:1] + tail[1:2] + tail[2:3]
        return scale, (jnp.max(tail[3:4, 0:128]) > 1.5).astype(jnp.int32)

    back = k.astype(F32)
    numbers = numbers_of(todo[0])
    for n, block in enumerate(todo):
        scale, far = numbers
        if n + 1 < len(todo):
            numbers = numbers_of(todo[n + 1])
        mixture = (
            (scale + (1.0 - back)) * green[2 * far].astype(F32)
            + (scale + back) * green[2 * far + 1].astype(F32)
        ).astype(BF16)
        weights = block[:NO, :]
        left = mul(weights, mixture).astype(BF16)
        yield mul_t(left, weights)


def blocks_of(refs):
    todo = []
    for ref in refs:
        todo += [ref.at[t] for t in range(2)] if len(ref.shape) == 3 else [ref]
    return todo


def first_kernel(place, own, near, shared, far, home, c1, c3, half, other, out, green, gsem):
    copies = [
        pltpu.make_async_copy(src, green.at[n], gsem.at[n])
        for n, src in enumerate((own, near, shared, far))
    ]
    for copy in copies:
        copy.start()
    for copy in copies:
        copy.wait()
    todo = blocks_of((home, c1, c3, half, other))
    for n, term in enumerate(add_terms(place[1], green, todo)):
        out[...] = term if n == 0 else out[...] + term


def last_kernel(
    place, green, start, s0, s1, s3, half, other, retarded, out, whole, acc, rsem
):
    k, sl = place[1], place[2]
    copies = [pltpu.make_async_copy(retarded.at[k, sl], whole, rsem.at[0])]
    todo = blocks_of((s0, s1, s3, half, other))
    for copy in copies:
        copy.start()
    for n, term in enumerate(add_terms(k, green, todo)):
        total = (start if n == 0 else acc)[...] + term
        if n == len(todo) - 1:
            out[...] = total.astype(BF16)
        else:
            acc[...] = total
    for copy in copies:
        copy.wait()


COST = pl.CostEstimate(flops=8 * 4 * NO**3, bytes_accessed=18 * NO * NO * 2, transcendentals=0)


def sandwich_first(place, greens, arrays):
    return pl.pallas_call(
        first_kernel,
        out_shape=[shape((NO, NO), F32), shape((4, NO, NO), BF16)],
        in_specs=[SMEM] + [VMEM] * 9,
        out_specs=[VMEM] * 2,
        scratch_shapes=[pltpu.SemaphoreType.DMA((4,))],
        compiler_params=PARAMS,
        cost_estimate=COST,
        name="sandwich_first",
    )(place, *greens, *arrays)


def sandwich_last(place, green, start, arrays, retarded):
    return pl.pallas_call(
        last_kernel,
        out_shape=[shape((NO, NO), BF16), shape((2, NO, NO), BF16)],
        in_specs=[SMEM] + [VMEM] * 7 + [HBM],
        out_specs=[VMEM] * 2,
        scratch_shapes=[pltpu.VMEM((NO, NO), F32), pltpu.SemaphoreType.DMA((1,))],
        compiler_params=PARAMS,
        cost_estimate=COST,
        name="sandwich_last",
    )(place, green, start, *arrays, retarded)


def update_kernel(place, weight, own, inner, outer, green, out):
    sl, c = place[2], place[4]
    beside = inner[...].astype(F32) + outer[...].astype(F32)
    combined = (own[...].astype(F32) + weight[sl] * beside).astype(BF16)
    a, b = green[0], green[1]
    a_side = mul_t(combined, a).astype(BF16)
    b_side = mul_t(combined, b).astype(BF16)
    real = mul(a, a_side) + mul(b, b_side)
    imag = mul(b, a_side) - mul(a, b_side)
    first = jnp.where(c == 0, real, -imag).astype(BF16)
    second = jnp.where(c == 0, imag, real).astype(BF16)
    for dest in range(8):
        rows = slice(dest * ROWS, (dest + 1) * ROWS)
        out[dest, 0] = first[rows]
        out[dest, 1] = second[rows]


def update(place, weight, own, inner, outer, green):
    return pl.pallas_call(
        update_kernel,
        out_shape=shape((8, 2, ROWS, NO), BF16),
        in_specs=[SMEM] * 2 + [VMEM] * 4,
        out_specs=VMEM,
        compiler_params=PARAMS,
        cost_estimate=pl.CostEstimate(
            flops=12 * NO**3, bytes_accessed=10 * NO * NO * 2, transcendentals=0
        ),
        name="update",
    )(place, weight, own, inner, outer, green)


def collect_kernel(place, pieces, out):
    b = place[3]
    for k in range(2):
        for parity in range(2):
            source = 2 * parity + k
            total = pieces[source].astype(F32) + pieces[source + 4].astype(F32)
            out[k, parity ^ b] = total


def collect(place, pieces):
    return pl.pallas_call(
        collect_kernel,
        out_shape=shape((2, 2, 2, ROWS, NO), F32),
        in_specs=[SMEM, VMEM],
        out_specs=VMEM,
        compiler_params=PARAMS,
        name="collect",
    )(place, pieces)


def shards(lesser, retarded, coupling, occupations, offsets, intersection):
    fr = lax.axis_index("freq")
    b = lax.axis_index("slab")
    y, k = fr >> 1, fr & 1
    x = (lax.axis_index("energy") >> 2) & 1
    place = jnp.stack([y, k, (y & 1) ^ b, b, y >> 1, x]).astype(jnp.int32)

    def flip(x, bits):
        return lax.ppermute(x, "freq", [(d, d ^ bits) for d in range(8)])

    count = lax.axis_size("energy")
    across = []
    for d in range(8):
        for e in range(count):
            target = e + 1 if d % 2 == 0 else e - 1
            if 0 <= target < count:
                across.append((d * count + e, d * count + target))

    packed, part, own, mine = prepare(place, occupations, offsets, coupling, lesser)
    half = flip(part, 4)
    other = lax.ppermute(half, "energy", [(e, e ^ 4) for e in range(count)])
    c1, c3 = flip(packed, 2), flip(packed, 6)
    near = lax.ppermute(own, ("freq", "energy"), across)
    far = lax.ppermute(mine, ("freq", "energy"), across)
    shared = flip(near, 1)
    swapped = [flip(x, 1) for x in (packed, c1, c3, half, other)]

    first, green = sandwich_first(
        place, [own, near, shared, far], [packed, c1, c3, half, other]
    )
    total, whole = sandwich_last(place, green, first, swapped, retarded)
    inner = flip(total, 2)
    edge = [(s * 8 + d, (1 - s) * 8 + d) for s in range(2) for d in range(8) if (d // 2) % 2]
    outer = lax.ppermute(total, ("slab", "freq"), edge)
    pieces = update(place, intersection, total, inner, outer, whole)
    return collect(place, lax.all_to_all(pieces, "freq", 0, 0))


def solution(mesh):
    return jax.shard_map(
        shards,
        mesh=mesh,
        in_specs=(
            P("energy", "slab", None, None, None),
            P("energy", "slab", None, None, None),
            P("freq", None, None),
            P("freq"),
            P("freq"),
            P("slab"),
        ),
        out_specs=P("energy", "slab", None, "freq", None),
        check_vma=False,
    )
```

```python
import functools
import jax
import jax.numpy as jnp
from jax import lax
from jax.experimental import pallas as pl
from jax.experimental.pallas import tpu as pltpu
from jax.sharding import PartitionSpec as P

NO = 512
ROWS = 64
TAIL = 16
F32 = jnp.float32
BF16 = jnp.bfloat16
MIB = 1 << 20
HBM = pl.BlockSpec(memory_space=pltpu.HBM)
SMEM = pl.BlockSpec(memory_space=pltpu.SMEM)
VMEM = pl.BlockSpec(memory_space=pltpu.VMEM)
PARAMS = pltpu.CompilerParams(vmem_limit_bytes=24 * MIB)


def shape(dims, kind):
    return jax.ShapeDtypeStruct(dims, kind)


def mul(a, b):
    return jnp.dot(a, b, preferred_element_type=F32)


def mul_t(a, b):
    return lax.dot_general(a, b, (((1,), (1,)), ((), ())), preferred_element_type=F32)


def prepare_kernel(
    place, occupations, offsets, coupling, lesser, packed, half, near, far, sem
):
    k, sl, c, x = place[1], place[2], place[4], place[5]
    copies = [
        pltpu.make_async_copy(lesser.at[1 - k, sl, c], near, sem.at[0]),
        pltpu.make_async_copy(lesser.at[k, sl, c], far, sem.at[1]),
        pltpu.make_async_copy(coupling.at[x], half.at[pl.ds(0, NO)], sem.at[2]),
    ]
    for t in range(2):
        copies.append(
            pltpu.make_async_copy(coupling.at[t], packed.at[t, pl.ds(0, NO)], sem.at[3 + t])
        )
    for copy in copies:
        copy.start()
    row = lax.broadcasted_iota(jnp.int32, (TAIL, NO), 0)

    def tail_of(t):
        whole = jnp.full((TAIL, NO), occupations[t], F32)
        high = whole.astype(BF16).astype(F32)
        middle = (whole - high).astype(BF16).astype(F32)
        low = whole - high - middle
        steps = jnp.full((TAIL, NO), offsets[t], jnp.int32).astype(F32)
        rows = jnp.where(row == 2, low, steps)
        return jnp.where(row == 0, high, jnp.where(row == 1, middle, rows)).astype(BF16)

    packed[0, NO:] = tail_of(0)
    packed[1, NO:] = tail_of(1)
    half[NO:] = tail_of(x)
    for copy in copies:
        copy.wait()


def prepare(place, occupations, offsets, coupling, lesser):
    block = (NO + TAIL, NO)
    return pl.pallas_call(
        prepare_kernel,
        out_shape=[shape((2, *block), BF16), shape(block, BF16)] + [shape((NO, NO), BF16)] * 2,
        in_specs=[SMEM] * 3 + [HBM] * 2,
        out_specs=[VMEM] * 4,
        scratch_shapes=[pltpu.SemaphoreType.DMA((5,))],
        compiler_params=pltpu.CompilerParams(vmem_limit_bytes=60 * MIB),
        name="prepare",
    )(place, occupations, offsets, coupling, lesser)


def add_terms(k, green, todo):
    def numbers_of(block):
        tail = block[NO:, :].astype(F32)
        scale = tail[0:1] + tail[1:2] + tail[2:3]
        return scale, (jnp.max(tail[3:4, 0:128]) > 1.5).astype(jnp.int32)

    back = k.astype(F32)
    numbers = numbers_of(todo[0])
    for n, block in enumerate(todo):
        scale, far = numbers
        if n + 1 < len(todo):
            numbers = numbers_of(todo[n + 1])
        mixture = (
            (scale + (1.0 - back)) * green[2 * far].astype(F32)
            + (scale + back) * green[2 * far + 1].astype(F32)
        ).astype(BF16)
        weights = block[:NO, :]
        left = mul(weights, mixture).astype(BF16)
        yield mul_t(left, weights)


def blocks_of(refs):
    todo = []
    for ref in refs:
        todo += [ref.at[t] for t in range(2)] if len(ref.shape) == 3 else [ref]
    return todo


def first_kernel(place, own, near, shared, far, c1, c3, half, other, out, green, gsem):
    copies = [
        pltpu.make_async_copy(src, green.at[n], gsem.at[n])
        for n, src in enumerate((own, near, shared, far))
    ]
    for copy in copies:
        copy.start()
    for copy in copies:
        copy.wait()
    todo = blocks_of((c1, c3, half, other))
    for n, term in enumerate(add_terms(place[1], green, todo)):
        out[...] = term if n == 0 else out[...] + term


def last_kernel(
    place, green, start, home, s0, s1, s3, half, other, retarded, out, whole, acc, rsem
):
    k, sl = place[1], place[2]
    copies = [pltpu.make_async_copy(retarded.at[k, sl], whole, rsem.at[0])]
    todo = blocks_of((home, s0, s1, s3, half, other))
    for copy in copies:
        copy.start()
    for n, term in enumerate(add_terms(k, green, todo)):
        total = (start if n == 0 else acc)[...] + term
        if n == len(todo) - 1:
            out[...] = total.astype(BF16)
        else:
            acc[...] = total
    for copy in copies:
        copy.wait()


def cost(count):
    return pl.CostEstimate(
        flops=count * 4 * NO**3, bytes_accessed=(count + 10) * NO * NO * 2, transcendentals=0
    )


def sandwich_first(place, greens, arrays):
    return pl.pallas_call(
        first_kernel,
        out_shape=[shape((NO, NO), F32), shape((4, NO, NO), BF16)],
        in_specs=[SMEM] + [VMEM] * 8,
        out_specs=[VMEM] * 2,
        scratch_shapes=[pltpu.SemaphoreType.DMA((4,))],
        compiler_params=PARAMS,
        cost_estimate=cost(6),
        name="sandwich_first",
    )(place, *greens, *arrays)


def sandwich_last(place, green, start, arrays, retarded):
    return pl.pallas_call(
        last_kernel,
        out_shape=[shape((NO, NO), BF16), shape((2, NO, NO), BF16)],
        in_specs=[SMEM] + [VMEM] * 8 + [HBM],
        out_specs=[VMEM] * 2,
        scratch_shapes=[pltpu.VMEM((NO, NO), F32), pltpu.SemaphoreType.DMA((1,))],
        compiler_params=PARAMS,
        cost_estimate=cost(10),
        name="sandwich_last",
    )(place, green, start, *arrays, retarded)


def update_kernel(place, weight, own, inner, outer, green, out):
    sl, c = place[2], place[4]
    beside = inner[...].astype(F32) + outer[...].astype(F32)
    combined = (own[...].astype(F32) + weight[sl] * beside).astype(BF16)
    a, b = green[0], green[1]
    a_side = mul_t(combined, a).astype(BF16)
    b_side = mul_t(combined, b).astype(BF16)
    real = mul(a, a_side) + mul(b, b_side)
    imag = mul(b, a_side) - mul(a, b_side)
    first = jnp.where(c == 0, real, -imag).astype(BF16)
    second = jnp.where(c == 0, imag, real).astype(BF16)
    for dest in range(8):
        rows = slice(dest * ROWS, (dest + 1) * ROWS)
        out[dest, 0] = first[rows]
        out[dest, 1] = second[rows]


def update(place, weight, own, inner, outer, green):
    return pl.pallas_call(
        update_kernel,
        out_shape=shape((8, 2, ROWS, NO), BF16),
        in_specs=[SMEM] * 2 + [VMEM] * 4,
        out_specs=VMEM,
        compiler_params=PARAMS,
        cost_estimate=pl.CostEstimate(
            flops=12 * NO**3, bytes_accessed=10 * NO * NO * 2, transcendentals=0
        ),
        name="update",
    )(place, weight, own, inner, outer, green)


def collect_kernel(place, pieces, out):
    b = place[3]
    for k in range(2):
        for parity in range(2):
            source = 2 * parity + k
            total = pieces[source].astype(F32) + pieces[source + 4].astype(F32)
            out[k, parity ^ b] = total


def collect(place, pieces):
    return pl.pallas_call(
        collect_kernel,
        out_shape=shape((2, 2, 2, ROWS, NO), F32),
        in_specs=[SMEM, VMEM],
        out_specs=VMEM,
        compiler_params=PARAMS,
        name="collect",
    )(place, pieces)


def shards(lesser, retarded, coupling, occupations, offsets, intersection):
    fr = lax.axis_index("freq")
    b = lax.axis_index("slab")
    y, k = fr >> 1, fr & 1
    x = (lax.axis_index("energy") >> 2) & 1
    place = jnp.stack([y, k, (y & 1) ^ b, b, y >> 1, x]).astype(jnp.int32)

    def flip(x, bits):
        return lax.ppermute(x, "freq", [(d, d ^ bits) for d in range(8)])

    count = lax.axis_size("energy")
    across = []
    for d in range(8):
        for e in range(count):
            target = e + 1 if d % 2 == 0 else e - 1
            if 0 <= target < count:
                across.append((d * count + e, d * count + target))

    packed, part, own, mine = prepare(place, occupations, offsets, coupling, lesser)
    half = flip(part, 4)
    near = lax.ppermute(own, ("freq", "energy"), across)
    half, near, packed = lax.optimization_barrier((half, near, packed))
    c1, c3 = flip(packed, 2), flip(packed, 6)
    far = lax.ppermute(mine, ("freq", "energy"), across)
    other = lax.ppermute(half, "energy", [(e, e ^ 4) for e in range(count)])
    own, shared = flip(mine, 1), flip(near, 1)
    swapped = [flip(x, 1) for x in (packed, c1, c3, half, other)]

    first, green = sandwich_first(place, [own, near, shared, far], [c1, c3, half, other])
    total, whole = sandwich_last(place, green, first, [packed, *swapped], retarded)
    inner = flip(total, 2)
    edge = [(s * 8 + d, (1 - s) * 8 + d) for s in range(2) for d in range(8) if (d // 2) % 2]
    outer = lax.ppermute(total, ("slab", "freq"), edge)
    pieces = update(place, intersection, total, inner, outer, whole)
    return collect(place, lax.all_to_all(pieces, "freq", 0, 0))


def solution(mesh):
    return jax.shard_map(
        shards,
        mesh=mesh,
        in_specs=(
            P("energy", "slab", None, None, None),
            P("energy", "slab", None, None, None),
            P("freq", None, None),
            P("freq"),
            P("freq"),
            P("slab"),
        ),
        out_specs=P("energy", "slab", None, "freq", None),
        check_vma=False,
    )
```

```python
import functools
import jax
import jax.numpy as jnp
from jax import lax
from jax.experimental import pallas as pl
from jax.experimental.pallas import tpu as pltpu
from jax.sharding import PartitionSpec as P

NO = 512
ROWS = 64
TAIL = 16
F32 = jnp.float32
BF16 = jnp.bfloat16
MIB = 1 << 20
HBM = pl.BlockSpec(memory_space=pltpu.HBM)
SMEM = pl.BlockSpec(memory_space=pltpu.SMEM)
VMEM = pl.BlockSpec(memory_space=pltpu.VMEM)
PARAMS = pltpu.CompilerParams(vmem_limit_bytes=24 * MIB)


def shape(dims, kind):
    return jax.ShapeDtypeStruct(dims, kind)


def mul(a, b):
    return jnp.dot(a, b, preferred_element_type=F32)


def mul_t(a, b):
    return lax.dot_general(a, b, (((1,), (1,)), ((), ())), preferred_element_type=F32)


def prepare_kernel(
    place, occupations, offsets, coupling, lesser, packed, half, mine, pair, sem
):
    k, sl, c, x = place[1], place[2], place[4], place[5]
    copies = [
        pltpu.make_async_copy(lesser.at[k, sl, c], mine, sem.at[0]),
        pltpu.make_async_copy(lesser.at[k, 1 - sl, c], pair, sem.at[1]),
        pltpu.make_async_copy(coupling.at[x], half.at[pl.ds(0, NO)], sem.at[2]),
    ]
    for t in range(2):
        copies.append(
            pltpu.make_async_copy(coupling.at[t], packed.at[t, pl.ds(0, NO)], sem.at[3 + t])
        )
    for copy in copies:
        copy.start()
    row = lax.broadcasted_iota(jnp.int32, (TAIL, NO), 0)

    def tail_of(t):
        whole = jnp.full((TAIL, NO), occupations[t], F32)
        high = whole.astype(BF16).astype(F32)
        middle = (whole - high).astype(BF16).astype(F32)
        low = whole - high - middle
        steps = jnp.full((TAIL, NO), offsets[t], jnp.int32).astype(F32)
        rows = jnp.where(row == 2, low, steps)
        return jnp.where(row == 0, high, jnp.where(row == 1, middle, rows)).astype(BF16)

    packed[0, NO:] = tail_of(0)
    packed[1, NO:] = tail_of(1)
    half[NO:] = tail_of(x)
    for copy in copies:
        copy.wait()


def prepare(place, occupations, offsets, coupling, lesser):
    block = (NO + TAIL, NO)
    return pl.pallas_call(
        prepare_kernel,
        out_shape=[shape((2, *block), BF16), shape(block, BF16)] + [shape((NO, NO), BF16)] * 2,
        in_specs=[SMEM] * 3 + [HBM] * 2,
        out_specs=[VMEM] * 4,
        scratch_shapes=[pltpu.SemaphoreType.DMA((5,))],
        compiler_params=pltpu.CompilerParams(vmem_limit_bytes=60 * MIB),
        name="prepare",
    )(place, occupations, offsets, coupling, lesser)


def mix_kernel(place, weight, mine, pair, cross, out):
    beside = pair[...].astype(F32) + cross[...].astype(F32)
    out[...] = (mine[...].astype(F32) + weight[place[2]] * beside).astype(BF16)


def mix(place, weight, mine, pair, cross):
    return pl.pallas_call(
        mix_kernel,
        out_shape=shape((NO, NO), BF16),
        in_specs=[SMEM] * 2 + [VMEM] * 3,
        out_specs=VMEM,
        compiler_params=PARAMS,
        name="mix",
    )(place, weight, mine, pair, cross)


def add_terms(k, green, todo):
    def numbers_of(block):
        tail = block[NO:, :].astype(F32)
        scale = tail[0:1] + tail[1:2] + tail[2:3]
        return scale, (jnp.max(tail[3:4, 0:128]) > 1.5).astype(jnp.int32)

    back = k.astype(F32)
    numbers = numbers_of(todo[0])
    for n, block in enumerate(todo):
        scale, far = numbers
        if n + 1 < len(todo):
            numbers = numbers_of(todo[n + 1])
        mixture = (
            (scale + (1.0 - back)) * green[2 * far].astype(F32)
            + (scale + back) * green[2 * far + 1].astype(F32)
        ).astype(BF16)
        weights = block[:NO, :]
        left = mul(weights, mixture).astype(BF16)
        yield mul_t(left, weights)


def blocks_of(refs):
    todo = []
    for ref in refs:
        todo += [ref.at[t] for t in range(2)] if len(ref.shape) == 3 else [ref]
    return todo


def first_kernel(place, own, near, shared, far, c1, c3, half, other, out, green, gsem):
    copies = [
        pltpu.make_async_copy(src, green.at[n], gsem.at[n])
        for n, src in enumerate((own, near, shared, far))
    ]
    for copy in copies:
        copy.start()
    for copy in copies:
        copy.wait()
    todo = blocks_of((c1, c3, half, other))
    for n, term in enumerate(add_terms(place[1], green, todo)):
        out[...] = term if n == 0 else out[...] + term


def last_kernel(
    place, green, start, home, s0, s1, s3, half, other, retarded, out, whole, acc, rsem
):
    k, sl, c = place[1], place[2], place[4]
    copy = pltpu.make_async_copy(retarded.at[k, sl], whole, rsem.at[0])
    copy.start()
    todo = blocks_of((home, s0, s1, s3, half, other))
    for n, term in enumerate(add_terms(k, green, todo)):
        acc[...] = (start if n == 0 else acc)[...] + term
    combined = acc[...].astype(BF16)
    copy.wait()
    a, b = whole[0], whole[1]
    a_side = mul_t(combined, a).astype(BF16)
    b_side = mul_t(combined, b).astype(BF16)
    real = mul(a, a_side) + mul(b, b_side)
    imag = mul(b, a_side) - mul(a, b_side)
    first = jnp.where(c == 0, real, -imag).astype(BF16)
    second = jnp.where(c == 0, imag, real).astype(BF16)
    for dest in range(8):
        rows = slice(dest * ROWS, (dest + 1) * ROWS)
        out[dest, 0] = first[rows]
        out[dest, 1] = second[rows]


def cost(count):
    return pl.CostEstimate(
        flops=count * 4 * NO**3, bytes_accessed=(count + 10) * NO * NO * 2, transcendentals=0
    )


def sandwich_first(place, greens, arrays):
    return pl.pallas_call(
        first_kernel,
        out_shape=[shape((NO, NO), F32), shape((4, NO, NO), BF16)],
        in_specs=[SMEM] + [VMEM] * 8,
        out_specs=[VMEM] * 2,
        scratch_shapes=[pltpu.SemaphoreType.DMA((4,))],
        compiler_params=PARAMS,
        cost_estimate=cost(6),
        name="sandwich_first",
    )(place, *greens, *arrays)


def sandwich_last(place, green, start, arrays, retarded):
    return pl.pallas_call(
        last_kernel,
        out_shape=shape((8, 2, ROWS, NO), BF16),
        in_specs=[SMEM] + [VMEM] * 8 + [HBM],
        out_specs=VMEM,
        scratch_shapes=[
            pltpu.VMEM((2, NO, NO), BF16),
            pltpu.VMEM((NO, NO), F32),
            pltpu.SemaphoreType.DMA((1,)),
        ],
        compiler_params=PARAMS,
        cost_estimate=cost(13),
        name="sandwich_last",
    )(place, green, start, *arrays, retarded)


def collect_kernel(place, pieces, out):
    b = place[3]
    for k in range(2):
        for parity in range(2):
            source = 2 * parity + k
            total = pieces[source].astype(F32) + pieces[source + 4].astype(F32)
            out[k, parity ^ b] = total


def collect(place, pieces):
    return pl.pallas_call(
        collect_kernel,
        out_shape=shape((2, 2, 2, ROWS, NO), F32),
        in_specs=[SMEM, VMEM],
        out_specs=VMEM,
        compiler_params=PARAMS,
        name="collect",
    )(place, pieces)


def shards(lesser, retarded, coupling, occupations, offsets, intersection):
    fr = lax.axis_index("freq")
    b = lax.axis_index("slab")
    y, k = fr >> 1, fr & 1
    x = (lax.axis_index("energy") >> 2) & 1
    place = jnp.stack([y, k, (y & 1) ^ b, b, y >> 1, x]).astype(jnp.int32)

    def flip(x, bits):
        return lax.ppermute(x, "freq", [(d, d ^ bits) for d in range(8)])

    count = lax.axis_size("energy")
    near_pairs, far_pairs = [], []
    for d in range(8):
        for e in range(count):
            for pairs, target, step in (
                (near_pairs, d ^ 1, 1 if d % 2 else -1),
                (far_pairs, d, -1 if d % 2 else 1),
            ):
                if 0 <= e + step < count:
                    pairs.append((d * count + e, target * count + e + step))

    packed, part, mine, pair = prepare(place, occupations, offsets, coupling, lesser)
    half = flip(part, 4)
    edge = [(s * 8 + d, (1 - s) * 8 + d) for s in range(2) for d in range(8) if (d // 2) % 2]
    cross = lax.ppermute(mine, ("slab", "freq"), edge)
    mixed = mix(place, intersection, mine, pair, cross)
    half, mixed, packed = lax.optimization_barrier((half, mixed, packed))
    c1, c3 = flip(packed, 2), flip(packed, 6)
    near = lax.ppermute(mixed, ("freq", "energy"), near_pairs)
    far = lax.ppermute(mixed, ("freq", "energy"), far_pairs)
    other = lax.ppermute(half, "energy", [(e, e ^ 4) for e in range(count)])
    own, shared = flip(mixed, 1), flip(near, 1)
    own, shared, far, packed = lax.optimization_barrier((own, shared, far, packed))
    swapped = [flip(x, 1) for x in (packed, c1, c3, half, other)]

    first, green = sandwich_first(place, [own, near, shared, far], [c1, c3, half, other])
    pieces = sandwich_last(place, green, first, [packed, *swapped], retarded)
    return collect(place, lax.all_to_all(pieces, "freq", 0, 0))


def solution(mesh):
    return jax.shard_map(
        shards,
        mesh=mesh,
        in_specs=(
            P("energy", "slab", None, None, None),
            P("energy", "slab", None, None, None),
            P("freq", None, None),
            P("freq"),
            P("freq"),
            P("slab"),
        ),
        out_specs=P("energy", "slab", None, "freq", None),
        check_vma=False,
    )
```

```python
import functools
import jax
import jax.numpy as jnp
from jax import lax
from jax.experimental import pallas as pl
from jax.experimental.pallas import tpu as pltpu
from jax.sharding import PartitionSpec as P

NO = 512
ROWS = 64
TAIL = 16
F32 = jnp.float32
BF16 = jnp.bfloat16
MIB = 1 << 20
HBM = pl.BlockSpec(memory_space=pltpu.HBM)
SMEM = pl.BlockSpec(memory_space=pltpu.SMEM)
VMEM = pl.BlockSpec(memory_space=pltpu.VMEM)
PARAMS = pltpu.CompilerParams(vmem_limit_bytes=24 * MIB)


def shape(dims, kind):
    return jax.ShapeDtypeStruct(dims, kind)


def mul(a, b):
    return jnp.dot(a, b, preferred_element_type=F32)


def mul_t(a, b):
    return lax.dot_general(a, b, (((1,), (1,)), ((), ())), preferred_element_type=F32)


def prepare_kernel(place, occupations, offsets, coupling, packed, half, sem):
    x = place[5]
    copies = [pltpu.make_async_copy(coupling.at[x], half.at[pl.ds(0, NO)], sem.at[2])]
    for t in range(2):
        copies.append(
            pltpu.make_async_copy(coupling.at[t], packed.at[t, pl.ds(0, NO)], sem.at[t])
        )
    for copy in copies:
        copy.start()
    row = lax.broadcasted_iota(jnp.int32, (TAIL, NO), 0)

    def tail_of(t):
        whole = jnp.full((TAIL, NO), occupations[t], F32)
        high = whole.astype(BF16).astype(F32)
        middle = (whole - high).astype(BF16).astype(F32)
        low = whole - high - middle
        steps = jnp.full((TAIL, NO), offsets[t], jnp.int32).astype(F32)
        rows = jnp.where(row == 2, low, steps)
        return jnp.where(row == 0, high, jnp.where(row == 1, middle, rows)).astype(BF16)

    packed[0, NO:] = tail_of(0)
    packed[1, NO:] = tail_of(1)
    half[NO:] = tail_of(x)
    for copy in copies:
        copy.wait()


def prepare(place, occupations, offsets, coupling):
    block = (NO + TAIL, NO)
    return pl.pallas_call(
        prepare_kernel,
        out_shape=[shape((2, *block), BF16), shape(block, BF16)],
        in_specs=[SMEM] * 3 + [HBM],
        out_specs=[VMEM] * 2,
        scratch_shapes=[pltpu.SemaphoreType.DMA((3,))],
        compiler_params=pltpu.CompilerParams(vmem_limit_bytes=60 * MIB),
        name="prepare",
    )(place, occupations, offsets, coupling)


def mix_kernel(place, weight, mine, pair, cross, out):
    beside = pair[...].astype(F32) + cross[...].astype(F32)
    out[...] = (mine[...].astype(F32) + weight[place[2]] * beside).astype(BF16)


def mix(place, weight, mine, pair, cross):
    return pl.pallas_call(
        mix_kernel,
        out_shape=shape((NO, NO), BF16),
        in_specs=[SMEM] * 2 + [VMEM] * 3,
        out_specs=VMEM,
        compiler_params=PARAMS,
        name="mix",
    )(place, weight, mine, pair, cross)


def add_terms(k, green, todo):
    def numbers_of(block):
        tail = block[NO:, :].astype(F32)
        scale = tail[0:1] + tail[1:2] + tail[2:3]
        return scale, (jnp.max(tail[3:4, 0:128]) > 1.5).astype(jnp.int32)

    back = k.astype(F32)
    numbers = numbers_of(todo[0])
    for n, block in enumerate(todo):
        scale, far = numbers
        if n + 1 < len(todo):
            numbers = numbers_of(todo[n + 1])
        mixture = (
            (scale + (1.0 - back)) * green[2 * far].astype(F32)
            + (scale + back) * green[2 * far + 1].astype(F32)
        ).astype(BF16)
        weights = block[:NO, :]
        left = mul(weights, mixture).astype(BF16)
        yield mul_t(left, weights)


def blocks_of(refs):
    todo = []
    for ref in refs:
        todo += [ref.at[t] for t in range(2)] if len(ref.shape) == 3 else [ref]
    return todo


def first_kernel(place, own, near, shared, far, c1, c3, half, other, out, green, gsem):
    copies = [
        pltpu.make_async_copy(src, green.at[n], gsem.at[n])
        for n, src in enumerate((own, near, shared, far))
    ]
    for copy in copies:
        copy.start()
    for copy in copies:
        copy.wait()
    todo = blocks_of((c1, c3, half, other))
    for n, term in enumerate(add_terms(place[1], green, todo)):
        out[...] = term if n == 0 else out[...] + term


def last_kernel(
    place, green, start, home, s0, s1, s3, half, other, retarded, out, whole, acc, rsem
):
    k, sl, c = place[1], place[2], place[4]
    copy = pltpu.make_async_copy(retarded.at[k, sl], whole, rsem.at[0])
    copy.start()
    todo = blocks_of((home, s0, s1, s3, half, other))
    for n, term in enumerate(add_terms(k, green, todo)):
        acc[...] = (start if n == 0 else acc)[...] + term
    combined = acc[...].astype(BF16)
    copy.wait()
    a, b = whole[0], whole[1]
    a_side = mul_t(combined, a).astype(BF16)
    b_side = mul_t(combined, b).astype(BF16)
    real = mul(a, a_side) + mul(b, b_side)
    imag = mul(b, a_side) - mul(a, b_side)
    first = jnp.where(c == 0, real, -imag).astype(BF16)
    second = jnp.where(c == 0, imag, real).astype(BF16)
    for dest in range(8):
        rows = slice(dest * ROWS, (dest + 1) * ROWS)
        out[dest, 0] = first[rows]
        out[dest, 1] = second[rows]


def cost(count):
    return pl.CostEstimate(
        flops=count * 4 * NO**3, bytes_accessed=(count + 10) * NO * NO * 2, transcendentals=0
    )


def sandwich_first(place, greens, arrays):
    return pl.pallas_call(
        first_kernel,
        out_shape=[shape((NO, NO), F32), shape((4, NO, NO), BF16)],
        in_specs=[SMEM] + [VMEM] * 8,
        out_specs=[VMEM] * 2,
        scratch_shapes=[pltpu.SemaphoreType.DMA((4,))],
        compiler_params=PARAMS,
        cost_estimate=cost(6),
        name="sandwich_first",
    )(place, *greens, *arrays)


def sandwich_last(place, green, start, arrays, retarded):
    return pl.pallas_call(
        last_kernel,
        out_shape=shape((8, 2, ROWS, NO), BF16),
        in_specs=[SMEM] + [VMEM] * 8 + [HBM],
        out_specs=VMEM,
        scratch_shapes=[
            pltpu.VMEM((2, NO, NO), BF16),
            pltpu.VMEM((NO, NO), F32),
            pltpu.SemaphoreType.DMA((1,)),
        ],
        compiler_params=PARAMS,
        cost_estimate=cost(13),
        name="sandwich_last",
    )(place, green, start, *arrays, retarded)


def collect_kernel(place, pieces, out):
    b = place[3]
    for k in range(2):
        for parity in range(2):
            source = 2 * parity + k
            total = pieces[source].astype(F32) + pieces[source + 4].astype(F32)
            out[k, parity ^ b] = total


def collect(place, pieces):
    return pl.pallas_call(
        collect_kernel,
        out_shape=shape((2, 2, 2, ROWS, NO), F32),
        in_specs=[SMEM, VMEM],
        out_specs=VMEM,
        compiler_params=PARAMS,
        name="collect",
    )(place, pieces)


def shards(lesser, retarded, coupling, occupations, offsets, intersection):
    fr = lax.axis_index("freq")
    b = lax.axis_index("slab")
    y, k = fr >> 1, fr & 1
    x = (lax.axis_index("energy") >> 2) & 1
    place = jnp.stack([y, k, (y & 1) ^ b, b, y >> 1, x]).astype(jnp.int32)

    def flip(x, bits):
        return lax.ppermute(x, "freq", [(d, d ^ bits) for d in range(8)])

    count = lax.axis_size("energy")
    near_pairs, far_pairs = [], []
    for d in range(8):
        for e in range(count):
            for pairs, target, step in (
                (near_pairs, d ^ 1, 1 if d % 2 else -1),
                (far_pairs, d, -1 if d % 2 else 1),
            ):
                if 0 <= e + step < count:
                    pairs.append((d * count + e, target * count + e + step))

    sl, c = (y & 1) ^ b, y >> 1
    mine, pair = lesser[k, sl, c], lesser[k, 1 - sl, c]
    edge = [(s * 8 + d, (1 - s) * 8 + d) for s in range(2) for d in range(8) if (d // 2) % 2]
    cross = lax.ppermute(mine, ("slab", "freq"), edge)
    packed, part = prepare(place, occupations, offsets, coupling)
    half = flip(part, 4)
    mixed = mix(place, intersection, mine, pair, cross)
    half, packed = lax.optimization_barrier((half, packed))
    c1, c3 = flip(packed, 2), flip(packed, 6)
    near = lax.ppermute(mixed, ("freq", "energy"), near_pairs)
    far = lax.ppermute(mixed, ("freq", "energy"), far_pairs)
    other = lax.ppermute(half, "energy", [(e, e ^ 4) for e in range(count)])
    own, shared = flip(mixed, 1), flip(near, 1)
    own, shared, far, packed, half, other = lax.optimization_barrier(
        (own, shared, far, packed, half, other)
    )
    swapped = [flip(x, 1) for x in (packed, c1, c3, half, other)]

    first, green = sandwich_first(place, [own, near, shared, far], [c1, c3, half, other])
    pieces = sandwich_last(place, green, first, [packed, *swapped], retarded)
    return collect(place, lax.all_to_all(pieces, "freq", 0, 0))


def solution(mesh):
    return jax.shard_map(
        shards,
        mesh=mesh,
        in_specs=(
            P("energy", "slab", None, None, None),
            P("energy", "slab", None, None, None),
            P("freq", None, None),
            P("freq"),
            P("freq"),
            P("slab"),
        ),
        out_specs=P("energy", "slab", None, "freq", None),
        check_vma=False,
    )
```

```python
import functools
import jax
import jax.numpy as jnp
from jax import lax
from jax.experimental import pallas as pl
from jax.experimental.pallas import tpu as pltpu
from jax.sharding import PartitionSpec as P

NO = 512
ROWS = 64
TAIL = 16
F32 = jnp.float32
BF16 = jnp.bfloat16
MIB = 1 << 20
HBM = pl.BlockSpec(memory_space=pltpu.HBM)
SMEM = pl.BlockSpec(memory_space=pltpu.SMEM)
VMEM = pl.BlockSpec(memory_space=pltpu.VMEM)
PARAMS = pltpu.CompilerParams(vmem_limit_bytes=24 * MIB)


def shape(dims, kind):
    return jax.ShapeDtypeStruct(dims, kind)


def mul(a, b):
    return jnp.dot(a, b, preferred_element_type=F32)


def mul_t(a, b):
    return lax.dot_general(a, b, (((1,), (1,)), ((), ())), preferred_element_type=F32)


def prepare_kernel(place, occupations, offsets, coupling, packed, half, sem):
    x = place[5]
    copies = [pltpu.make_async_copy(coupling.at[x], half.at[pl.ds(0, NO)], sem.at[2])]
    for t in range(2):
        copies.append(
            pltpu.make_async_copy(coupling.at[t], packed.at[t, pl.ds(0, NO)], sem.at[t])
        )
    for copy in copies:
        copy.start()
    row = lax.broadcasted_iota(jnp.int32, (TAIL, NO), 0)

    def tail_of(t):
        whole = jnp.full((TAIL, NO), occupations[t], F32)
        high = whole.astype(BF16).astype(F32)
        middle = (whole - high).astype(BF16).astype(F32)
        low = whole - high - middle
        steps = jnp.full((TAIL, NO), offsets[t], jnp.int32).astype(F32)
        rows = jnp.where(row == 2, low, steps)
        return jnp.where(row == 0, high, jnp.where(row == 1, middle, rows)).astype(BF16)

    packed[0, NO:] = tail_of(0)
    packed[1, NO:] = tail_of(1)
    half[NO:] = tail_of(x)
    for copy in copies:
        copy.wait()


def prepare(place, occupations, offsets, coupling):
    block = (NO + TAIL, NO)
    return pl.pallas_call(
        prepare_kernel,
        out_shape=[shape((2, *block), BF16), shape(block, BF16)],
        in_specs=[SMEM] * 3 + [HBM],
        out_specs=[VMEM] * 2,
        scratch_shapes=[pltpu.SemaphoreType.DMA((3,))],
        compiler_params=pltpu.CompilerParams(vmem_limit_bytes=60 * MIB),
        name="prepare",
    )(place, occupations, offsets, coupling)


def mix_kernel(place, weight, mine, pair, cross, out):
    beside = pair[...].astype(F32) + cross[...].astype(F32)
    out[...] = (mine[...].astype(F32) + weight[place[2]] * beside).astype(BF16)


def mix(place, weight, mine, pair, cross):
    return pl.pallas_call(
        mix_kernel,
        out_shape=shape((NO, NO), BF16),
        in_specs=[SMEM] * 2 + [VMEM] * 3,
        out_specs=VMEM,
        compiler_params=PARAMS,
        name="mix",
    )(place, weight, mine, pair, cross)


def add_terms(k, green, todo):
    def numbers_of(block):
        tail = block[NO:, :].astype(F32)
        scale = tail[0:1] + tail[1:2] + tail[2:3]
        return scale, (jnp.max(tail[3:4, 0:128]) > 1.5).astype(jnp.int32)

    back = k.astype(F32)
    numbers = numbers_of(todo[0])
    for n, block in enumerate(todo):
        scale, far = numbers
        if n + 1 < len(todo):
            numbers = numbers_of(todo[n + 1])
        mixture = (
            (scale + (1.0 - back)) * green[2 * far].astype(F32)
            + (scale + back) * green[2 * far + 1].astype(F32)
        ).astype(BF16)
        weights = block[:NO, :]
        left = mul(weights, mixture).astype(BF16)
        yield mul_t(left, weights)


def blocks_of(refs):
    todo = []
    for ref in refs:
        todo += [ref.at[t] for t in range(2)] if len(ref.shape) == 3 else [ref]
    return todo


def first_kernel(place, own, near, shared, far, c1, c3, half, other, out, green, gsem):
    copies = [
        pltpu.make_async_copy(src, green.at[n], gsem.at[n])
        for n, src in enumerate((own, near, shared, far))
    ]
    for copy in copies:
        copy.start()
    for copy in copies:
        copy.wait()
    todo = blocks_of((c1, c3, half, other))
    for n, term in enumerate(add_terms(place[1], green, todo)):
        out[...] = term if n == 0 else out[...] + term


def last_kernel(
    place, green, start, home, s0, s1, s3, half, other, retarded, out, whole, acc, rsem
):
    k, sl, c = place[1], place[2], place[4]
    copy = pltpu.make_async_copy(retarded.at[k, sl], whole, rsem.at[0])
    copy.start()
    todo = blocks_of((home, s0, s1, s3, half, other))
    for n, term in enumerate(add_terms(k, green, todo)):
        acc[...] = (start if n == 0 else acc)[...] + term
    combined = acc[...].astype(BF16)
    copy.wait()
    a, b = whole[0], whole[1]
    a_side = mul_t(combined, a).astype(BF16)
    b_side = mul_t(combined, b).astype(BF16)
    real = mul(a, a_side) + mul(b, b_side)
    imag = mul(b, a_side) - mul(a, b_side)
    first = jnp.where(c == 0, real, -imag).astype(BF16)
    second = jnp.where(c == 0, imag, real).astype(BF16)
    for dest in range(8):
        rows = slice(dest * ROWS, (dest + 1) * ROWS)
        out[dest, 0] = first[rows]
        out[dest, 1] = second[rows]


def cost(count):
    return pl.CostEstimate(
        flops=count * 4 * NO**3, bytes_accessed=(count + 10) * NO * NO * 2, transcendentals=0
    )


def sandwich_first(place, greens, arrays):
    return pl.pallas_call(
        first_kernel,
        out_shape=[shape((NO, NO), F32), shape((4, NO, NO), BF16)],
        in_specs=[SMEM] + [VMEM] * 8,
        out_specs=[VMEM] * 2,
        scratch_shapes=[pltpu.SemaphoreType.DMA((4,))],
        compiler_params=PARAMS,
        cost_estimate=cost(6),
        name="sandwich_first",
    )(place, *greens, *arrays)


def sandwich_last(place, green, start, arrays, retarded):
    return pl.pallas_call(
        last_kernel,
        out_shape=shape((8, 2, ROWS, NO), BF16),
        in_specs=[SMEM] + [VMEM] * 8 + [HBM],
        out_specs=VMEM,
        scratch_shapes=[
            pltpu.VMEM((2, NO, NO), BF16),
            pltpu.VMEM((NO, NO), F32),
            pltpu.SemaphoreType.DMA((1,)),
        ],
        compiler_params=PARAMS,
        cost_estimate=cost(13),
        name="sandwich_last",
    )(place, green, start, *arrays, retarded)


def collect_kernel(place, pieces, out):
    b = place[3]
    for k in range(2):
        for parity in range(2):
            source = 2 * parity + k
            total = pieces[source].astype(F32) + pieces[source + 4].astype(F32)
            out[k, parity ^ b] = total


def collect(place, pieces):
    return pl.pallas_call(
        collect_kernel,
        out_shape=shape((2, 2, 2, ROWS, NO), F32),
        in_specs=[SMEM, VMEM],
        out_specs=VMEM,
        compiler_params=PARAMS,
        name="collect",
    )(place, pieces)


def shards(lesser, retarded, coupling, occupations, offsets, intersection):
    fr = lax.axis_index("freq")
    b = lax.axis_index("slab")
    y, k = fr >> 1, fr & 1
    x = (lax.axis_index("energy") >> 2) & 1
    place = jnp.stack([y, k, (y & 1) ^ b, b, y >> 1, x]).astype(jnp.int32)

    def flip(x, bits):
        return lax.ppermute(x, "freq", [(d, d ^ bits) for d in range(8)])

    count = lax.axis_size("energy")
    near_pairs, far_pairs = [], []
    for d in range(8):
        for e in range(count):
            for pairs, target, step in (
                (near_pairs, d ^ 1, 1 if d % 2 else -1),
                (far_pairs, d, -1 if d % 2 else 1),
            ):
                if 0 <= e + step < count:
                    pairs.append((d * count + e, target * count + e + step))

    sl, c = (y & 1) ^ b, y >> 1
    mine, pair = lesser[k, sl, c], lesser[k, 1 - sl, c]
    edge = [(s * 8 + d, (1 - s) * 8 + d) for s in range(2) for d in range(8) if (d // 2) % 2]
    cross = lax.ppermute(mine, ("slab", "freq"), edge)
    packed, part = prepare(place, occupations, offsets, coupling)
    half = flip(part, 4)
    mixed = mix(place, intersection, mine, pair, cross)
    near = lax.ppermute(mixed, ("freq", "energy"), near_pairs)
    own, shared = flip(mixed, 1), flip(near, 1)
    own, mixed, half, packed = lax.optimization_barrier((own, mixed, half, packed))
    c1, c3 = flip(packed, 2), flip(packed, 6)
    far = lax.ppermute(mixed, ("freq", "energy"), far_pairs)
    other = lax.ppermute(half, "energy", [(e, e ^ 4) for e in range(count)])
    own, shared, far, packed, half, other = lax.optimization_barrier(
        (own, shared, far, packed, half, other)
    )
    swapped = [flip(x, 1) for x in (packed, c1, c3, half, other)]

    first, green = sandwich_first(place, [own, near, shared, far], [c1, c3, half, other])
    pieces = sandwich_last(place, green, first, [packed, *swapped], retarded)
    return collect(place, lax.all_to_all(pieces, "freq", 0, 0))


def solution(mesh):
    return jax.shard_map(
        shards,
        mesh=mesh,
        in_specs=(
            P("energy", "slab", None, None, None),
            P("energy", "slab", None, None, None),
            P("freq", None, None),
            P("freq"),
            P("freq"),
            P("slab"),
        ),
        out_specs=P("energy", "slab", None, "freq", None),
        check_vma=False,
    )
```

```python
import functools
import jax
import jax.numpy as jnp
from jax import lax
from jax.experimental import pallas as pl
from jax.experimental.pallas import tpu as pltpu
from jax.sharding import PartitionSpec as P

NO = 512
ROWS = 64
TAIL = 16
F32 = jnp.float32
BF16 = jnp.bfloat16
MIB = 1 << 20
HBM = pl.BlockSpec(memory_space=pltpu.HBM)
SMEM = pl.BlockSpec(memory_space=pltpu.SMEM)
VMEM = pl.BlockSpec(memory_space=pltpu.VMEM)
PARAMS = pltpu.CompilerParams(vmem_limit_bytes=24 * MIB)


def shape(dims, kind):
    return jax.ShapeDtypeStruct(dims, kind)


def mul(a, b):
    return jnp.dot(a, b, preferred_element_type=F32)


def mul_t(a, b):
    return lax.dot_general(a, b, (((1,), (1,)), ((), ())), preferred_element_type=F32)


def prepare_kernel(place, occupations, offsets, coupling, packed, half, sem):
    x = place[5]
    copies = [pltpu.make_async_copy(coupling.at[x], half.at[pl.ds(0, NO)], sem.at[2])]
    for t in range(2):
        copies.append(
            pltpu.make_async_copy(coupling.at[t], packed.at[t, pl.ds(0, NO)], sem.at[t])
        )
    for copy in copies:
        copy.start()
    row = lax.broadcasted_iota(jnp.int32, (TAIL, NO), 0)

    def tail_of(t):
        whole = jnp.full((TAIL, NO), occupations[t], F32)
        high = whole.astype(BF16).astype(F32)
        middle = (whole - high).astype(BF16).astype(F32)
        low = whole - high - middle
        steps = jnp.full((TAIL, NO), offsets[t], jnp.int32).astype(F32)
        rows = jnp.where(row == 2, low, steps)
        return jnp.where(row == 0, high, jnp.where(row == 1, middle, rows)).astype(BF16)

    packed[0, NO:] = tail_of(0)
    packed[1, NO:] = tail_of(1)
    half[NO:] = tail_of(x)
    for copy in copies:
        copy.wait()


def prepare(place, occupations, offsets, coupling):
    block = (NO + TAIL, NO)
    return pl.pallas_call(
        prepare_kernel,
        out_shape=[shape((2, *block), BF16), shape(block, BF16)],
        in_specs=[SMEM] * 3 + [HBM],
        out_specs=[VMEM] * 2,
        scratch_shapes=[pltpu.SemaphoreType.DMA((3,))],
        compiler_params=pltpu.CompilerParams(vmem_limit_bytes=60 * MIB),
        name="prepare",
    )(place, occupations, offsets, coupling)


def mix_kernel(place, weight, mine, pair, cross, out):
    beside = pair[...].astype(F32) + cross[...].astype(F32)
    out[...] = (mine[...].astype(F32) + weight[place[2]] * beside).astype(BF16)


def mix(place, weight, mine, pair, cross):
    return pl.pallas_call(
        mix_kernel,
        out_shape=shape((NO, NO), BF16),
        in_specs=[SMEM] * 2 + [VMEM] * 3,
        out_specs=VMEM,
        compiler_params=PARAMS,
        name="mix",
    )(place, weight, mine, pair, cross)


def add_terms(k, green, todo):
    def numbers_of(block):
        tail = block[NO:, :].astype(F32)
        scale = tail[0:1] + tail[1:2] + tail[2:3]
        return scale, (jnp.max(tail[3:4, 0:128]) > 1.5).astype(jnp.int32)

    back = k.astype(F32)
    numbers = numbers_of(todo[0])
    for n, block in enumerate(todo):
        scale, far = numbers
        if n + 1 < len(todo):
            numbers = numbers_of(todo[n + 1])
        mixture = (
            (scale + (1.0 - back)) * green[2 * far].astype(F32)
            + (scale + back) * green[2 * far + 1].astype(F32)
        ).astype(BF16)
        weights = block[:NO, :]
        left = mul(weights, mixture).astype(BF16)
        yield mul_t(left, weights)


def blocks_of(refs):
    todo = []
    for ref in refs:
        todo += [ref.at[t] for t in range(2)] if len(ref.shape) == 3 else [ref]
    return todo


def first_kernel(place, own, near, shared, far, c1, c3, half, other, out, green, gsem):
    copies = [
        pltpu.make_async_copy(src, green.at[n], gsem.at[n])
        for n, src in enumerate((own, near, shared, far))
    ]
    for copy in copies:
        copy.start()
    for copy in copies:
        copy.wait()
    todo = blocks_of((c1, c3, half, other))
    for n, term in enumerate(add_terms(place[1], green, todo)):
        out[...] = term if n == 0 else out[...] + term


def last_kernel(
    place, green, start, home, s0, s1, s3, half, other, retarded, out, whole, acc, rsem
):
    k, sl, c = place[1], place[2], place[4]
    copy = pltpu.make_async_copy(retarded.at[k, sl], whole, rsem.at[0])
    copy.start()
    todo = blocks_of((home, s0, s1, s3, half, other))
    for n, term in enumerate(add_terms(k, green, todo)):
        acc[...] = (start if n == 0 else acc)[...] + term
    combined = acc[...].astype(BF16)
    copy.wait()
    a, b = whole[0], whole[1]
    a_side = mul_t(combined, a).astype(BF16)
    b_side = mul_t(combined, b).astype(BF16)
    real = mul(a, a_side) + mul(b, b_side)
    imag = mul(b, a_side) - mul(a, b_side)
    first = jnp.where(c == 0, real, -imag).astype(BF16)
    second = jnp.where(c == 0, imag, real).astype(BF16)
    for dest in range(8):
        rows = slice(dest * ROWS, (dest + 1) * ROWS)
        out[dest, 0] = first[rows]
        out[dest, 1] = second[rows]


def cost(count):
    return pl.CostEstimate(
        flops=count * 4 * NO**3, bytes_accessed=(count + 10) * NO * NO * 2, transcendentals=0
    )


def sandwich_first(place, greens, arrays):
    return pl.pallas_call(
        first_kernel,
        out_shape=[shape((NO, NO), F32), shape((4, NO, NO), BF16)],
        in_specs=[SMEM] + [VMEM] * 8,
        out_specs=[VMEM] * 2,
        scratch_shapes=[pltpu.SemaphoreType.DMA((4,))],
        compiler_params=PARAMS,
        cost_estimate=cost(6),
        name="sandwich_first",
    )(place, *greens, *arrays)


def sandwich_last(place, green, start, arrays, retarded):
    return pl.pallas_call(
        last_kernel,
        out_shape=shape((8, 2, ROWS, NO), BF16),
        in_specs=[SMEM] + [VMEM] * 8 + [HBM],
        out_specs=VMEM,
        scratch_shapes=[
            pltpu.VMEM((2, NO, NO), BF16),
            pltpu.VMEM((NO, NO), F32),
            pltpu.SemaphoreType.DMA((1,)),
        ],
        compiler_params=PARAMS,
        cost_estimate=cost(13),
        name="sandwich_last",
    )(place, green, start, *arrays, retarded)


def collect_kernel(place, pieces, out):
    b = place[3]
    for k in range(2):
        for parity in range(2):
            source = 2 * parity + k
            total = pieces[source].astype(F32) + pieces[source + 4].astype(F32)
            out[k, parity ^ b] = total


def collect(place, pieces):
    return pl.pallas_call(
        collect_kernel,
        out_shape=shape((2, 2, 2, ROWS, NO), F32),
        in_specs=[SMEM, VMEM],
        out_specs=VMEM,
        compiler_params=PARAMS,
        name="collect",
    )(place, pieces)


def shards(lesser, retarded, coupling, occupations, offsets, intersection):
    fr = lax.axis_index("freq")
    b = lax.axis_index("slab")
    y, k = fr >> 1, fr & 1
    x = (lax.axis_index("energy") >> 2) & 1
    place = jnp.stack([y, k, (y & 1) ^ b, b, y >> 1, x]).astype(jnp.int32)

    def flip(x, bits):
        return lax.ppermute(x, "freq", [(d, d ^ bits) for d in range(8)])

    count = lax.axis_size("energy")
    near_pairs, far_pairs = [], []
    for d in range(8):
        for e in range(count):
            for pairs, target, step in (
                (near_pairs, d ^ 1, 1 if d % 2 else -1),
                (far_pairs, d, -1 if d % 2 else 1),
            ):
                if 0 <= e + step < count:
                    pairs.append((d * count + e, target * count + e + step))

    sl, c = (y & 1) ^ b, y >> 1
    mine, pair = lesser[k, sl, c], lesser[k, 1 - sl, c]
    edge = [(s * 8 + d, (1 - s) * 8 + d) for s in range(2) for d in range(8) if (d // 2) % 2]
    cross = lax.ppermute(mine, ("slab", "freq"), edge)
    packed, part = prepare(place, occupations, offsets, coupling)
    half = flip(part, 4)
    mixed = mix(place, intersection, mine, pair, cross)
    mixed, packed = lax.optimization_barrier((mixed, packed))
    near = lax.ppermute(mixed, ("freq", "energy"), near_pairs)
    far = lax.ppermute(mixed, ("freq", "energy"), far_pairs)
    c1, c3 = flip(packed, 2), flip(packed, 6)
    near, mixed = lax.optimization_barrier((near, mixed))
    own, shared = flip(mixed, 1), flip(near, 1)
    other = lax.ppermute(half, "energy", [(e, e ^ 4) for e in range(count)])
    own, shared, far, packed, half, other = lax.optimization_barrier(
        (own, shared, far, packed, half, other)
    )
    swapped = [flip(x, 1) for x in (packed, c1, c3, half, other)]

    first, green = sandwich_first(place, [own, near, shared, far], [c1, c3, half, other])
    pieces = sandwich_last(place, green, first, [packed, *swapped], retarded)
    return collect(place, lax.all_to_all(pieces, "freq", 0, 0))


def solution(mesh):
    return jax.shard_map(
        shards,
        mesh=mesh,
        in_specs=(
            P("energy", "slab", None, None, None),
            P("energy", "slab", None, None, None),
            P("freq", None, None),
            P("freq"),
            P("freq"),
            P("slab"),
        ),
        out_specs=P("energy", "slab", None, "freq", None),
        check_vma=False,
    )
```

```python
import functools
import jax
import jax.numpy as jnp
from jax import lax
from jax.experimental import pallas as pl
from jax.experimental.pallas import tpu as pltpu
from jax.sharding import PartitionSpec as P

NO = 512
ROWS = 64
TAIL = 16
F32 = jnp.float32
BF16 = jnp.bfloat16
MIB = 1 << 20
HBM = pl.BlockSpec(memory_space=pltpu.HBM)
SMEM = pl.BlockSpec(memory_space=pltpu.SMEM)
VMEM = pl.BlockSpec(memory_space=pltpu.VMEM)
PARAMS = pltpu.CompilerParams(vmem_limit_bytes=24 * MIB)


def shape(dims, kind):
    return jax.ShapeDtypeStruct(dims, kind)


def mul(a, b):
    return jnp.dot(a, b, preferred_element_type=F32)


def mul_t(a, b):
    return lax.dot_general(a, b, (((1,), (1,)), ((), ())), preferred_element_type=F32)


def prepare_kernel(place, occupations, offsets, coupling, packed, half, sem):
    x = place[5]
    copies = [pltpu.make_async_copy(coupling.at[x], half.at[pl.ds(0, NO)], sem.at[2])]
    for t in range(2):
        copies.append(
            pltpu.make_async_copy(coupling.at[t], packed.at[t, pl.ds(0, NO)], sem.at[t])
        )
    for copy in copies:
        copy.start()
    row = lax.broadcasted_iota(jnp.int32, (TAIL, NO), 0)

    def tail_of(t):
        whole = jnp.full((TAIL, NO), occupations[t], F32)
        high = whole.astype(BF16).astype(F32)
        middle = (whole - high).astype(BF16).astype(F32)
        low = whole - high - middle
        steps = jnp.full((TAIL, NO), offsets[t], jnp.int32).astype(F32)
        rows = jnp.where(row == 2, low, steps)
        return jnp.where(row == 0, high, jnp.where(row == 1, middle, rows)).astype(BF16)

    packed[0, NO:] = tail_of(0)
    packed[1, NO:] = tail_of(1)
    half[NO:] = tail_of(x)
    for copy in copies:
        copy.wait()


def prepare(place, occupations, offsets, coupling):
    block = (NO + TAIL, NO)
    return pl.pallas_call(
        prepare_kernel,
        out_shape=[shape((2, *block), BF16), shape(block, BF16)],
        in_specs=[SMEM] * 3 + [HBM],
        out_specs=[VMEM] * 2,
        scratch_shapes=[pltpu.SemaphoreType.DMA((3,))],
        compiler_params=pltpu.CompilerParams(vmem_limit_bytes=60 * MIB),
        name="prepare",
    )(place, occupations, offsets, coupling)


def mix_kernel(place, weight, mine, pair, top, bottom, out):
    for cross, first in ((top, 0), (bottom, NO // 2)):
        rows = pl.ds(first, NO // 2)
        beside = pair[rows].astype(F32) + cross[...].astype(F32)
        out[rows] = (mine[rows].astype(F32) + weight[place[2]] * beside).astype(BF16)


def mix(place, weight, mine, pair, top, bottom):
    return pl.pallas_call(
        mix_kernel,
        out_shape=shape((NO, NO), BF16),
        in_specs=[SMEM] * 2 + [VMEM] * 4,
        out_specs=VMEM,
        compiler_params=PARAMS,
        name="mix",
    )(place, weight, mine, pair, top, bottom)


def add_terms(k, green, todo):
    def numbers_of(block):
        tail = block[NO:, :].astype(F32)
        scale = tail[0:1] + tail[1:2] + tail[2:3]
        return scale, (jnp.max(tail[3:4, 0:128]) > 1.5).astype(jnp.int32)

    back = k.astype(F32)
    numbers = numbers_of(todo[0])
    for n, block in enumerate(todo):
        scale, far = numbers
        if n + 1 < len(todo):
            numbers = numbers_of(todo[n + 1])
        mixture = (
            (scale + (1.0 - back)) * green[2 * far].astype(F32)
            + (scale + back) * green[2 * far + 1].astype(F32)
        ).astype(BF16)
        weights = block[:NO, :]
        left = mul(weights, mixture).astype(BF16)
        yield mul_t(left, weights)


def blocks_of(refs):
    todo = []
    for ref in refs:
        todo += [ref.at[t] for t in range(2)] if len(ref.shape) == 3 else [ref]
    return todo


def first_kernel(place, own, near, shared, far, home, c1, c3, half, other, out, green, gsem):
    copies = [
        pltpu.make_async_copy(src, green.at[n], gsem.at[n])
        for n, src in enumerate((own, near, shared, far))
    ]
    for copy in copies:
        copy.start()
    for copy in copies:
        copy.wait()
    todo = blocks_of((home, c1, c3, half, other))
    for n, term in enumerate(add_terms(place[1], green, todo)):
        out[...] = term if n == 0 else out[...] + term


def last_kernel(
    place, green, start, s0, s1, s3, half, other, retarded, out, whole, acc, rsem
):
    k, sl, c = place[1], place[2], place[4]
    copy = pltpu.make_async_copy(retarded.at[k, sl], whole, rsem.at[0])
    copy.start()
    todo = blocks_of((s0, s1, s3, half, other))
    for n, term in enumerate(add_terms(k, green, todo)):
        acc[...] = (start if n == 0 else acc)[...] + term
    combined = acc[...].astype(BF16)
    copy.wait()
    a, b = whole[0], whole[1]
    a_side = mul_t(combined, a).astype(BF16)
    b_side = mul_t(combined, b).astype(BF16)
    real = mul(a, a_side) + mul(b, b_side)
    imag = mul(b, a_side) - mul(a, b_side)
    first = jnp.where(c == 0, real, -imag).astype(BF16)
    second = jnp.where(c == 0, imag, real).astype(BF16)
    for dest in range(8):
        rows = slice(dest * ROWS, (dest + 1) * ROWS)
        out[dest, 0] = first[rows]
        out[dest, 1] = second[rows]


def cost(count):
    return pl.CostEstimate(
        flops=count * 4 * NO**3, bytes_accessed=(count + 10) * NO * NO * 2, transcendentals=0
    )


def sandwich_first(place, greens, arrays):
    return pl.pallas_call(
        first_kernel,
        out_shape=[shape((NO, NO), F32), shape((4, NO, NO), BF16)],
        in_specs=[SMEM] + [VMEM] * 9,
        out_specs=[VMEM] * 2,
        scratch_shapes=[pltpu.SemaphoreType.DMA((4,))],
        compiler_params=PARAMS,
        cost_estimate=cost(8),
        name="sandwich_first",
    )(place, *greens, *arrays)


def sandwich_last(place, green, start, arrays, retarded):
    return pl.pallas_call(
        last_kernel,
        out_shape=shape((8, 2, ROWS, NO), BF16),
        in_specs=[SMEM] + [VMEM] * 7 + [HBM],
        out_specs=VMEM,
        scratch_shapes=[
            pltpu.VMEM((2, NO, NO), BF16),
            pltpu.VMEM((NO, NO), F32),
            pltpu.SemaphoreType.DMA((1,)),
        ],
        compiler_params=PARAMS,
        cost_estimate=cost(11),
        name="sandwich_last",
    )(place, green, start, *arrays, retarded)


def collect_kernel(place, pieces, out):
    b = place[3]
    for k in range(2):
        for parity in range(2):
            source = 2 * parity + k
            total = pieces[source].astype(F32) + pieces[source + 4].astype(F32)
            out[k, parity ^ b] = total


def collect(place, pieces):
    return pl.pallas_call(
        collect_kernel,
        out_shape=shape((2, 2, 2, ROWS, NO), F32),
        in_specs=[SMEM, VMEM],
        out_specs=VMEM,
        compiler_params=PARAMS,
        name="collect",
    )(place, pieces)


def shards(lesser, retarded, coupling, occupations, offsets, intersection):
    fr = lax.axis_index("freq")
    b = lax.axis_index("slab")
    y, k = fr >> 1, fr & 1
    x = (lax.axis_index("energy") >> 2) & 1
    place = jnp.stack([y, k, (y & 1) ^ b, b, y >> 1, x]).astype(jnp.int32)

    def flip(x, bits):
        return lax.ppermute(x, "freq", [(d, d ^ bits) for d in range(8)])

    count = lax.axis_size("energy")
    near_pairs, far_pairs = [], []
    for d in range(8):
        for e in range(count):
            for pairs, target, step in (
                (near_pairs, d ^ 1, 1 if d % 2 else -1),
                (far_pairs, d, -1 if d % 2 else 1),
            ):
                if 0 <= e + step < count:
                    pairs.append((d * count + e, target * count + e + step))

    sl, c = (y & 1) ^ b, y >> 1
    mine, pair = lesser[k, sl, c], lesser[k, 1 - sl, c]
    odd = [d for d in range(8) if d & 2]
    upper = [(s * 8 + d, (1 - s) * 8 + d) for s in range(2) for d in odd]
    lower = [(s * 8 + (d ^ 2), (1 - s) * 8 + d) for s in range(2) for d in odd]
    rim = lesser[k, 1 - b, c]
    top = lax.ppermute(rim[: NO // 2], ("slab", "freq"), upper)
    bottom = lax.ppermute(rim[NO // 2 :], ("slab", "freq"), lower)
    packed, part = prepare(place, occupations, offsets, coupling)
    half = flip(part, 4)
    mixed = mix(place, intersection, mine, pair, top, bottom)
    mixed, packed = lax.optimization_barrier((mixed, packed))
    near = lax.ppermute(mixed, ("freq", "energy"), near_pairs)
    far = lax.ppermute(mixed, ("freq", "energy"), far_pairs)
    c1, c3 = flip(packed, 2), flip(packed, 6)
    near, mixed = lax.optimization_barrier((near, mixed))
    own, shared = flip(mixed, 1), flip(near, 1)
    other = lax.ppermute(half, "energy", [(e, e ^ 4) for e in range(count)])
    own, shared, far, packed, half, other = lax.optimization_barrier(
        (own, shared, far, packed, half, other)
    )
    swapped = [flip(x, 1) for x in (packed, c1, c3, half, other)]

    first, green = sandwich_first(place, [own, near, shared, far], [packed, c1, c3, half, other])
    pieces = sandwich_last(place, green, first, swapped, retarded)
    return collect(place, lax.all_to_all(pieces, "freq", 0, 0))


def solution(mesh):
    return jax.shard_map(
        shards,
        mesh=mesh,
        in_specs=(
            P("energy", "slab", None, None, None),
            P("energy", "slab", None, None, None),
            P("freq", None, None),
            P("freq"),
            P("freq"),
            P("slab"),
        ),
        out_specs=P("energy", "slab", None, "freq", None),
        check_vma=False,
    )
```

```python
import functools
import jax
import jax.numpy as jnp
from jax import lax
from jax.experimental import pallas as pl
from jax.experimental.pallas import tpu as pltpu
from jax.sharding import PartitionSpec as P

NO = 512
ROWS = 64
TAIL = 16
F32 = jnp.float32
BF16 = jnp.bfloat16
MIB = 1 << 20
HBM = pl.BlockSpec(memory_space=pltpu.HBM)
SMEM = pl.BlockSpec(memory_space=pltpu.SMEM)
VMEM = pl.BlockSpec(memory_space=pltpu.VMEM)
PARAMS = pltpu.CompilerParams(vmem_limit_bytes=24 * MIB)


def shape(dims, kind):
    return jax.ShapeDtypeStruct(dims, kind)


def mul(a, b):
    return jnp.dot(a, b, preferred_element_type=F32)


def mul_t(a, b):
    return lax.dot_general(a, b, (((1,), (1,)), ((), ())), preferred_element_type=F32)


def place():
    device, b = lax.axis_index("freq"), lax.axis_index("slab")
    y, k = device >> 1, device & 1
    return y, k, (y & 1) ^ b, b, y >> 1, (lax.axis_index("energy") >> 2) & 1


def prepare_kernel(occupations, offsets, coupling, packed, half, blocks, sem):
    x = place()[5]
    copies = [
        pltpu.make_async_copy(coupling.at[t], blocks.at[t, pl.ds(0, NO)], sem.at[t])
        for t in range(2)
    ]
    for copy in copies:
        copy.start()
    row = lax.broadcasted_iota(jnp.int32, (TAIL, NO), 0)
    for t in range(2):
        whole = jnp.full((TAIL, NO), occupations[t], F32)
        high = whole.astype(BF16).astype(F32)
        middle = (whole - high).astype(BF16).astype(F32)
        low = whole - high - middle
        steps = jnp.full((TAIL, NO), offsets[t], jnp.int32).astype(F32)
        rows = jnp.where(row == 2, low, steps)
        rows = jnp.where(row == 0, high, jnp.where(row == 1, middle, rows))
        blocks[t, NO:] = rows.astype(BF16)
    for copy in copies:
        copy.wait()
    copies = [
        pltpu.make_async_copy(blocks.at[x], half, sem.at[2]),
        pltpu.make_async_copy(blocks, packed, sem.at[3]),
    ]
    for copy in copies:
        copy.start()
    for copy in copies:
        copy.wait()


def prepare(occupations, offsets, coupling):
    block = (NO + TAIL, NO)
    return pl.pallas_call(
        prepare_kernel,
        out_shape=[shape((2, *block), BF16), shape(block, BF16)],
        in_specs=[SMEM] * 2 + [HBM],
        out_specs=[HBM] * 2,
        scratch_shapes=[pltpu.VMEM((2, *block), BF16), pltpu.SemaphoreType.DMA((4,))],
        compiler_params=pltpu.CompilerParams(vmem_limit_bytes=60 * MIB),
        name="prepare",
    )(occupations, offsets, coupling)


def mix_kernel(weight, mine, pair, top, bottom, out):
    scale = weight[place()[2]]
    for cross, first in ((top, 0), (bottom, NO // 2)):
        rows = pl.ds(first, NO // 2)
        beside = pair[rows].astype(F32) + cross[...].astype(F32)
        out[rows] = (mine[rows].astype(F32) + scale * beside).astype(BF16)


def mix(weight, mine, pair, top, bottom):
    return pl.pallas_call(
        mix_kernel,
        out_shape=shape((NO, NO), BF16),
        in_specs=[SMEM] + [VMEM] * 4,
        out_specs=VMEM,
        compiler_params=PARAMS,
        name="mix",
    )(weight, mine, pair, top, bottom)


def add_terms(k, green, todo):
    def numbers_of(block):
        tail = block[NO:, :].astype(F32)
        scale = tail[0:1] + tail[1:2] + tail[2:3]
        return scale, (jnp.max(tail[3:4, 0:128]) > 1.5).astype(jnp.int32)

    back = k.astype(F32)
    numbers = numbers_of(todo[0])
    for n, block in enumerate(todo):
        scale, far = numbers
        if n + 1 < len(todo):
            numbers = numbers_of(todo[n + 1])
        mixture = (
            (scale + (1.0 - back)) * green[2 * far].astype(F32)
            + (scale + back) * green[2 * far + 1].astype(F32)
        ).astype(BF16)
        weights = block[:NO, :]
        left = mul(weights, mixture).astype(BF16)
        yield mul_t(left, weights)


def blocks_of(refs):
    todo = []
    for ref in refs:
        todo += [ref.at[t] for t in range(2)] if len(ref.shape) == 3 else [ref]
    return todo


def first_kernel(own, near, shared, far, home, c1, c3, half, other, out, green, gsem):
    copies = [
        pltpu.make_async_copy(src, green.at[n], gsem.at[n])
        for n, src in enumerate((own, near, shared, far))
    ]
    for copy in copies:
        copy.start()
    for copy in copies:
        copy.wait()
    todo = blocks_of((home, c1, c3, half, other))
    for n, term in enumerate(add_terms(place()[1], green, todo)):
        out[...] = term if n == 0 else out[...] + term


def last_kernel(
    green, start, s0, s1, s3, half, other, retarded, out, whole, acc, rsem
):
    _, k, sl, _, c, _ = place()
    copy = pltpu.make_async_copy(retarded.at[k, sl], whole, rsem.at[0])
    copy.start()
    todo = blocks_of((s0, s1, s3, half, other))
    for n, term in enumerate(add_terms(k, green, todo)):
        acc[...] = (start if n == 0 else acc)[...] + term
    combined = acc[...].astype(BF16)
    copy.wait()
    a, b = whole[0], whole[1]
    a_side = mul_t(combined, a).astype(BF16)
    b_side = mul_t(combined, b).astype(BF16)
    real = mul(a, a_side) + mul(b, b_side)
    imag = mul(b, a_side) - mul(a, b_side)
    first = jnp.where(c == 0, real, -imag).astype(BF16)
    second = jnp.where(c == 0, imag, real).astype(BF16)
    for dest in range(8):
        rows = slice(dest * ROWS, (dest + 1) * ROWS)
        out[dest, 0] = first[rows]
        out[dest, 1] = second[rows]


def cost(count):
    return pl.CostEstimate(
        flops=count * 4 * NO**3, bytes_accessed=(count + 10) * NO * NO * 2, transcendentals=0
    )


def sandwich_first(greens, arrays):
    return pl.pallas_call(
        first_kernel,
        out_shape=[shape((NO, NO), F32), shape((4, NO, NO), BF16)],
        in_specs=[VMEM] * 9,
        out_specs=[VMEM] * 2,
        scratch_shapes=[pltpu.SemaphoreType.DMA((4,))],
        compiler_params=PARAMS,
        cost_estimate=cost(8),
        name="sandwich_first",
    )(*greens, *arrays)


def sandwich_last(green, start, arrays, retarded):
    return pl.pallas_call(
        last_kernel,
        out_shape=shape((8, 2, ROWS, NO), BF16),
        in_specs=[VMEM] * 7 + [HBM],
        out_specs=VMEM,
        scratch_shapes=[
            pltpu.VMEM((2, NO, NO), BF16),
            pltpu.VMEM((NO, NO), F32),
            pltpu.SemaphoreType.DMA((1,)),
        ],
        compiler_params=PARAMS,
        cost_estimate=cost(11),
        name="sandwich_last",
    )(green, start, *arrays, retarded)


def collect_kernel(pieces, out, total, sem):
    b = place()[3]
    copies = []
    for n in range(4):
        k, parity = n % 2, n // 2
        total[n] = pieces[n].astype(F32) + pieces[n + 4].astype(F32)
        copies.append(pltpu.make_async_copy(total.at[n], out.at[k, parity ^ b], sem.at[n]))
        copies[-1].start()
    for copy in copies:
        copy.wait()


def collect(pieces):
    return pl.pallas_call(
        collect_kernel,
        out_shape=shape((2, 2, 2, ROWS, NO), F32),
        in_specs=[VMEM],
        out_specs=HBM,
        scratch_shapes=[pltpu.VMEM((4, 2, ROWS, NO), F32), pltpu.SemaphoreType.DMA((4,))],
        compiler_params=PARAMS,
        name="collect",
    )(pieces)


def shards(lesser, retarded, coupling, occupations, offsets, intersection):
    _, k, sl, b, c, _ = place()

    def flip(x, bits):
        return lax.ppermute(x, "freq", [(d, d ^ bits) for d in range(8)])

    count = lax.axis_size("energy")
    near_pairs, far_pairs = [], []
    for d in range(8):
        for e in range(count):
            for pairs, target, step in (
                (near_pairs, d ^ 1, 1 if d % 2 else -1),
                (far_pairs, d, -1 if d % 2 else 1),
            ):
                if 0 <= e + step < count:
                    pairs.append((d * count + e, target * count + e + step))

    mine, pair = lesser[k, sl, c], lesser[k, 1 - sl, c]
    odd = [d for d in range(8) if d & 2]
    upper = [(s * 8 + d, (1 - s) * 8 + d) for s in range(2) for d in odd]
    lower = [(s * 8 + (d ^ 2), (1 - s) * 8 + d) for s in range(2) for d in odd]
    rim = lesser[k, 1 - b, c]
    top = lax.ppermute(rim[: NO // 2], ("slab", "freq"), upper)
    bottom = lax.ppermute(rim[NO // 2 :], ("slab", "freq"), lower)
    packed, part = prepare(occupations, offsets, coupling)
    half = flip(part, 4)
    mixed = mix(intersection, mine, pair, top, bottom)
    mixed, packed = lax.optimization_barrier((mixed, packed))
    near = lax.ppermute(mixed, ("freq", "energy"), near_pairs)
    far = lax.ppermute(mixed, ("freq", "energy"), far_pairs)
    c1, c3 = flip(packed, 2), flip(packed, 6)
    near, mixed = lax.optimization_barrier((near, mixed))
    own, shared = flip(mixed, 1), flip(near, 1)
    other = lax.ppermute(half, "energy", [(e, e ^ 4) for e in range(count)])
    own, shared, far, packed, half, other = lax.optimization_barrier(
        (own, shared, far, packed, half, other)
    )
    swapped = [flip(x, 1) for x in (packed, c1, c3, half, other)]

    first, green = sandwich_first([own, near, shared, far], [packed, c1, c3, half, other])
    pieces = sandwich_last(green, first, swapped, retarded)
    return collect(lax.all_to_all(pieces, "freq", 0, 0))


def solution(mesh):
    return jax.shard_map(
        shards,
        mesh=mesh,
        in_specs=(
            P("energy", "slab", None, None, None),
            P("energy", "slab", None, None, None),
            P("freq", None, None),
            P("freq"),
            P("freq"),
            P("slab"),
        ),
        out_specs=P("energy", "slab", None, "freq", None),
        check_vma=False,
    )
```

```python
import functools
import jax
import jax.numpy as jnp
from jax import lax
from jax.experimental import pallas as pl
from jax.experimental.pallas import tpu as pltpu
from jax.sharding import PartitionSpec as P

NO = 512
ROWS = 64
TAIL = 16
F32 = jnp.float32
BF16 = jnp.bfloat16
MIB = 1 << 20
HBM = pl.BlockSpec(memory_space=pltpu.HBM)
SMEM = pl.BlockSpec(memory_space=pltpu.SMEM)
VMEM = pl.BlockSpec(memory_space=pltpu.VMEM)
PARAMS = pltpu.CompilerParams(vmem_limit_bytes=24 * MIB)


def shape(dims, kind):
    return jax.ShapeDtypeStruct(dims, kind)


def mul(a, b):
    return jnp.dot(a, b, preferred_element_type=F32)


def mul_t(a, b):
    return lax.dot_general(a, b, (((1,), (1,)), ((), ())), preferred_element_type=F32)


def place():
    device, b = lax.axis_index("freq"), lax.axis_index("slab")
    y, k = device >> 1, device & 1
    return y, k, (y & 1) ^ b, b, y >> 1, (lax.axis_index("energy") >> 2) & 1


def prepare_kernel(occupations, offsets, coupling, packed, half, blocks, sem):
    x = place()[5]
    copies = [
        pltpu.make_async_copy(coupling.at[t], blocks.at[t, pl.ds(0, NO)], sem.at[t])
        for t in range(2)
    ]
    for copy in copies:
        copy.start()
    row = lax.broadcasted_iota(jnp.int32, (TAIL, NO), 0)
    for t in range(2):
        whole = jnp.full((TAIL, NO), occupations[t], F32)
        high = whole.astype(BF16).astype(F32)
        middle = (whole - high).astype(BF16).astype(F32)
        low = whole - high - middle
        steps = jnp.full((TAIL, NO), offsets[t], jnp.int32).astype(F32)
        rows = jnp.where(row == 2, low, steps)
        rows = jnp.where(row == 0, high, jnp.where(row == 1, middle, rows))
        blocks[t, NO:] = rows.astype(BF16)
    for copy in copies:
        copy.wait()
    copies = [
        pltpu.make_async_copy(blocks.at[x], half, sem.at[2]),
        pltpu.make_async_copy(blocks, packed, sem.at[3]),
    ]
    for copy in copies:
        copy.start()
    for copy in copies:
        copy.wait()


def prepare(occupations, offsets, coupling):
    block = (NO + TAIL, NO)
    return pl.pallas_call(
        prepare_kernel,
        out_shape=[shape((2, *block), BF16), shape(block, BF16)],
        in_specs=[SMEM] * 2 + [HBM],
        out_specs=[HBM] * 2,
        scratch_shapes=[pltpu.VMEM((2, *block), BF16), pltpu.SemaphoreType.DMA((4,))],
        compiler_params=pltpu.CompilerParams(vmem_limit_bytes=60 * MIB),
        name="prepare",
    )(occupations, offsets, coupling)


def mix_kernel(weight, mine, pair, top, bottom, out):
    scale = weight[place()[2]]
    for cross, first in ((top, 0), (bottom, NO // 2)):
        rows = pl.ds(first, NO // 2)
        beside = pair[rows].astype(F32) + cross[...].astype(F32)
        out[rows] = (mine[rows].astype(F32) + scale * beside).astype(BF16)


def mix(weight, mine, pair, top, bottom):
    return pl.pallas_call(
        mix_kernel,
        out_shape=shape((NO, NO), BF16),
        in_specs=[SMEM] + [VMEM] * 4,
        out_specs=VMEM,
        compiler_params=PARAMS,
        name="mix",
    )(weight, mine, pair, top, bottom)


def add_terms(k, green, todo):
    def numbers_of(block):
        tail = block[NO:, :].astype(F32)
        scale = tail[0:1] + tail[1:2] + tail[2:3]
        return scale, (jnp.max(tail[3:4, 0:128]) > 1.5).astype(jnp.int32)

    back = k.astype(F32)
    numbers = numbers_of(todo[0])
    for n, block in enumerate(todo):
        scale, far = numbers
        if n + 1 < len(todo):
            numbers = numbers_of(todo[n + 1])
        mixture = (
            (scale + (1.0 - back)) * green[2 * far].astype(F32)
            + (scale + back) * green[2 * far + 1].astype(F32)
        ).astype(BF16)
        weights = block[:NO, :]
        left = mul(weights, mixture).astype(BF16)
        yield mul_t(left, weights)


def blocks_of(refs):
    todo = []
    for ref in refs:
        todo += [ref.at[t] for t in range(2)] if len(ref.shape) == 3 else [ref]
    return todo


def first_kernel(own, near, shared, far, home, c1, c3, half, other, out, green, gsem):
    copies = [
        pltpu.make_async_copy(src, green.at[n], gsem.at[n])
        for n, src in enumerate((own, near, shared, far))
    ]
    for copy in copies:
        copy.start()
    for copy in copies:
        copy.wait()
    todo = blocks_of((home, c1, c3, half, other))
    for n, term in enumerate(add_terms(place()[1], green, todo)):
        out[...] = term if n == 0 else out[...] + term


def last_kernel(
    green, start, s0, s1, s3, half, other, retarded, out, whole, acc, rsem
):
    _, k, sl, _, c, _ = place()
    copy = pltpu.make_async_copy(retarded.at[k, sl], whole, rsem.at[0])
    copy.start()
    todo = blocks_of((s0, s1, s3, half, other))
    for n, term in enumerate(add_terms(k, green, todo)):
        acc[...] = (start if n == 0 else acc)[...] + term
    combined = acc[...].astype(BF16)
    copy.wait()
    a, b = whole[0], whole[1]
    a_side = mul_t(combined, a).astype(BF16)
    b_side = mul_t(combined, b).astype(BF16)
    real = mul(a, a_side) + mul(b, b_side)
    imag = mul(b, a_side) - mul(a, b_side)
    first = jnp.where(c == 0, real, -imag).astype(BF16)
    second = jnp.where(c == 0, imag, real).astype(BF16)
    for dest in range(8):
        rows = slice(dest * ROWS, (dest + 1) * ROWS)
        out[dest, 0] = first[rows]
        out[dest, 1] = second[rows]


def cost(count):
    return pl.CostEstimate(
        flops=count * 4 * NO**3, bytes_accessed=(count + 10) * NO * NO * 2, transcendentals=0
    )


def sandwich_first(greens, arrays):
    return pl.pallas_call(
        first_kernel,
        out_shape=[shape((NO, NO), F32), shape((4, NO, NO), BF16)],
        in_specs=[VMEM] * 9,
        out_specs=[VMEM] * 2,
        scratch_shapes=[pltpu.SemaphoreType.DMA((4,))],
        compiler_params=PARAMS,
        cost_estimate=cost(8),
        name="sandwich_first",
    )(*greens, *arrays)


def sandwich_last(green, start, arrays, retarded):
    return pl.pallas_call(
        last_kernel,
        out_shape=shape((8, 2, ROWS, NO), BF16),
        in_specs=[VMEM] * 7 + [HBM],
        out_specs=VMEM,
        scratch_shapes=[
            pltpu.VMEM((2, NO, NO), BF16),
            pltpu.VMEM((NO, NO), F32),
            pltpu.SemaphoreType.DMA((1,)),
        ],
        compiler_params=PARAMS,
        cost_estimate=cost(11),
        name="sandwich_last",
    )(green, start, *arrays, retarded)


def collect_kernel(pieces, out, total, sem):
    b = place()[3]
    copies = []
    for n in range(4):
        k, parity = n % 2, n // 2
        total[n] = pieces[n].astype(F32) + pieces[n + 4].astype(F32)
        copies.append(pltpu.make_async_copy(total.at[n], out.at[k, parity ^ b], sem.at[n]))
        copies[-1].start()
    for copy in copies:
        copy.wait()


def collect(pieces):
    return pl.pallas_call(
        collect_kernel,
        out_shape=shape((2, 2, 2, ROWS, NO), F32),
        in_specs=[VMEM],
        out_specs=HBM,
        scratch_shapes=[pltpu.VMEM((4, 2, ROWS, NO), F32), pltpu.SemaphoreType.DMA((4,))],
        compiler_params=PARAMS,
        name="collect",
    )(pieces)


def shards(lesser, retarded, coupling, occupations, offsets, intersection):
    _, k, sl, b, c, _ = place()

    def flip(x, bits):
        return lax.ppermute(x, "freq", [(d, d ^ bits) for d in range(8)])

    count = lax.axis_size("energy")
    near_pairs, far_pairs = [], []
    for d in range(8):
        for e in range(count):
            for pairs, target, step in (
                (near_pairs, d ^ 1, 1 if d % 2 else -1),
                (far_pairs, d, -1 if d % 2 else 1),
            ):
                if 0 <= e + step < count:
                    pairs.append((d * count + e, target * count + e + step))

    mine, pair = lesser[k, sl, c], lesser[k, 1 - sl, c]
    odd = [d for d in range(8) if d & 2]
    upper = [(s * 8 + d, (1 - s) * 8 + d) for s in range(2) for d in odd]
    lower = [(s * 8 + (d ^ 2), (1 - s) * 8 + d) for s in range(2) for d in odd]
    rim = lesser[k, 1 - b, c]
    top = lax.ppermute(rim[: NO // 2], ("slab", "freq"), upper)
    bottom = lax.ppermute(rim[NO // 2 :], ("slab", "freq"), lower)
    packed, part = prepare(occupations, offsets, coupling)
    half = flip(part, 4)
    mixed = mix(intersection, mine, pair, top, bottom)
    mixed, packed = lax.optimization_barrier((mixed, packed))
    near = lax.ppermute(mixed, ("freq", "energy"), near_pairs)
    c1, c3 = flip(packed, 2), flip(packed, 6)
    half, mixed = lax.optimization_barrier((half, mixed))
    far = lax.ppermute(mixed, ("freq", "energy"), far_pairs)
    other = lax.ppermute(half, "energy", [(e, e ^ 4) for e in range(count)])
    shared = flip(near, 1)
    other, shared, mixed = lax.optimization_barrier((other, shared, mixed))
    own = flip(mixed, 1)
    own, shared, far, packed, half, other = lax.optimization_barrier(
        (own, shared, far, packed, half, other)
    )
    swapped = [flip(x, 1) for x in (packed, c1, c3, half, other)]

    first, green = sandwich_first([own, near, shared, far], [packed, c1, c3, half, other])
    pieces = sandwich_last(green, first, swapped, retarded)
    return collect(lax.all_to_all(pieces, "freq", 0, 0))


def solution(mesh):
    return jax.shard_map(
        shards,
        mesh=mesh,
        in_specs=(
            P("energy", "slab", None, None, None),
            P("energy", "slab", None, None, None),
            P("freq", None, None),
            P("freq"),
            P("freq"),
            P("slab"),
        ),
        out_specs=P("energy", "slab", None, "freq", None),
        check_vma=False,
    )
```

```python
import functools
import jax
import jax.numpy as jnp
from jax import lax
from jax.experimental import pallas as pl
from jax.experimental.pallas import tpu as pltpu
from jax.sharding import PartitionSpec as P

NO = 512
ROWS = 64
TAIL = 16
F32 = jnp.float32
BF16 = jnp.bfloat16
MIB = 1 << 20
HBM = pl.BlockSpec(memory_space=pltpu.HBM)
SMEM = pl.BlockSpec(memory_space=pltpu.SMEM)
VMEM = pl.BlockSpec(memory_space=pltpu.VMEM)
PARAMS = pltpu.CompilerParams(vmem_limit_bytes=24 * MIB)


def shape(dims, kind):
    return jax.ShapeDtypeStruct(dims, kind)


def mul(a, b):
    return jnp.dot(a, b, preferred_element_type=F32)


def mul_t(a, b):
    return lax.dot_general(a, b, (((1,), (1,)), ((), ())), preferred_element_type=F32)


def place():
    device, b = lax.axis_index("freq"), lax.axis_index("slab")
    y, k = device >> 1, device & 1
    return y, k, (y & 1) ^ b, b, y >> 1, (lax.axis_index("energy") >> 2) & 1


def prepare_kernel(occupations, offsets, coupling, packed, half, blocks, sem):
    x = place()[5]
    copies = [
        pltpu.make_async_copy(coupling.at[t], blocks.at[t, pl.ds(0, NO)], sem.at[t])
        for t in range(2)
    ]
    for copy in copies:
        copy.start()
    row = lax.broadcasted_iota(jnp.int32, (TAIL, NO), 0)
    for t in range(2):
        whole = jnp.full((TAIL, NO), occupations[t], F32)
        high = whole.astype(BF16).astype(F32)
        middle = (whole - high).astype(BF16).astype(F32)
        low = whole - high - middle
        steps = jnp.full((TAIL, NO), offsets[t], jnp.int32).astype(F32)
        rows = jnp.where(row == 2, low, steps)
        rows = jnp.where(row == 0, high, jnp.where(row == 1, middle, rows))
        blocks[t, NO:] = rows.astype(BF16)
    for copy in copies:
        copy.wait()
    copies = [
        pltpu.make_async_copy(blocks.at[x], half, sem.at[2]),
        pltpu.make_async_copy(blocks, packed, sem.at[3]),
    ]
    for copy in copies:
        copy.start()
    for copy in copies:
        copy.wait()


def prepare(occupations, offsets, coupling):
    block = (NO + TAIL, NO)
    return pl.pallas_call(
        prepare_kernel,
        out_shape=[shape((2, *block), BF16), shape(block, BF16)],
        in_specs=[SMEM] * 2 + [HBM],
        out_specs=[HBM] * 2,
        scratch_shapes=[pltpu.VMEM((2, *block), BF16), pltpu.SemaphoreType.DMA((4,))],
        compiler_params=pltpu.CompilerParams(vmem_limit_bytes=60 * MIB),
        name="prepare",
    )(occupations, offsets, coupling)


def mix_kernel(weight, mine, pair, top, bottom, out):
    scale = weight[place()[2]]
    for cross, first in ((top, 0), (bottom, NO // 2)):
        rows = pl.ds(first, NO // 2)
        beside = pair[rows].astype(F32) + cross[...].astype(F32)
        out[rows] = (mine[rows].astype(F32) + scale * beside).astype(BF16)


def mix(weight, mine, pair, top, bottom):
    return pl.pallas_call(
        mix_kernel,
        out_shape=shape((NO, NO), BF16),
        in_specs=[SMEM] + [VMEM] * 4,
        out_specs=VMEM,
        compiler_params=PARAMS,
        name="mix",
    )(weight, mine, pair, top, bottom)


def add_terms(k, green, todo):
    def numbers_of(block):
        tail = block[NO:, :].astype(F32)
        scale = tail[0:1] + tail[1:2] + tail[2:3]
        return scale, (jnp.max(tail[3:4, 0:128]) > 1.5).astype(jnp.int32)

    back = k.astype(F32)
    numbers = numbers_of(todo[0])
    for n, block in enumerate(todo):
        scale, far = numbers
        if n + 1 < len(todo):
            numbers = numbers_of(todo[n + 1])
        mixture = (
            (scale + (1.0 - back)) * green[2 * far].astype(F32)
            + (scale + back) * green[2 * far + 1].astype(F32)
        ).astype(BF16)
        weights = block[:NO, :]
        left = mul(weights, mixture).astype(BF16)
        yield mul_t(left, weights)


def blocks_of(refs):
    todo = []
    for ref in refs:
        todo += [ref.at[t] for t in range(2)] if len(ref.shape) == 3 else [ref]
    return todo


def first_kernel(own, near, shared, far, home, c1, c3, half, other, out, green, gsem):
    copies = [
        pltpu.make_async_copy(src, green.at[n], gsem.at[n])
        for n, src in enumerate((own, near, shared, far))
    ]
    for copy in copies:
        copy.start()
    for copy in copies:
        copy.wait()
    todo = blocks_of((home, c1, c3, half, other))
    for n, term in enumerate(add_terms(place()[1], green, todo)):
        out[...] = term if n == 0 else out[...] + term


def last_kernel(
    green, start, s0, s1, s3, half, other, retarded, out, whole, acc, rsem
):
    _, k, sl, _, c, _ = place()
    copy = pltpu.make_async_copy(retarded.at[k, sl], whole, rsem.at[0])
    copy.start()
    todo = blocks_of((s0, s1, s3, half, other))
    for n, term in enumerate(add_terms(k, green, todo)):
        acc[...] = (start if n == 0 else acc)[...] + term
    combined = acc[...].astype(BF16)
    copy.wait()
    a, b = whole[0], whole[1]
    a_side = mul_t(combined, a).astype(BF16)
    b_side = mul_t(combined, b).astype(BF16)
    real = mul(a, a_side) + mul(b, b_side)
    imag = mul(b, a_side) - mul(a, b_side)
    first = jnp.where(c == 0, real, -imag).astype(BF16)
    second = jnp.where(c == 0, imag, real).astype(BF16)
    for dest in range(8):
        rows = slice(dest * ROWS, (dest + 1) * ROWS)
        out[dest, 0] = first[rows]
        out[dest, 1] = second[rows]


def cost(count):
    return pl.CostEstimate(
        flops=count * 4 * NO**3, bytes_accessed=(count + 10) * NO * NO * 2, transcendentals=0
    )


def sandwich_first(greens, arrays):
    return pl.pallas_call(
        first_kernel,
        out_shape=[shape((NO, NO), F32), shape((4, NO, NO), BF16)],
        in_specs=[VMEM] * 9,
        out_specs=[VMEM] * 2,
        scratch_shapes=[pltpu.SemaphoreType.DMA((4,))],
        compiler_params=PARAMS,
        cost_estimate=cost(8),
        name="sandwich_first",
    )(*greens, *arrays)


def sandwich_last(green, start, arrays, retarded):
    return pl.pallas_call(
        last_kernel,
        out_shape=shape((8, 2, ROWS, NO), BF16),
        in_specs=[VMEM] * 7 + [HBM],
        out_specs=VMEM,
        scratch_shapes=[
            pltpu.VMEM((2, NO, NO), BF16),
            pltpu.VMEM((NO, NO), F32),
            pltpu.SemaphoreType.DMA((1,)),
        ],
        compiler_params=PARAMS,
        cost_estimate=cost(11),
        name="sandwich_last",
    )(green, start, *arrays, retarded)


def collect_kernel(pieces, out, total, sem):
    b = place()[3]
    copies = []
    for n in range(4):
        k, parity = n % 2, n // 2
        total[n] = pieces[n].astype(F32) + pieces[n + 4].astype(F32)
        copies.append(pltpu.make_async_copy(total.at[n], out.at[k, parity ^ b], sem.at[n]))
        copies[-1].start()
    for copy in copies:
        copy.wait()


def collect(pieces):
    return pl.pallas_call(
        collect_kernel,
        out_shape=shape((2, 2, 2, ROWS, NO), F32),
        in_specs=[VMEM],
        out_specs=HBM,
        scratch_shapes=[pltpu.VMEM((4, 2, ROWS, NO), F32), pltpu.SemaphoreType.DMA((4,))],
        compiler_params=PARAMS,
        name="collect",
    )(pieces)


def shards(lesser, retarded, coupling, occupations, offsets, intersection):
    _, k, sl, b, c, _ = place()

    def flip(x, bits):
        return lax.ppermute(x, "freq", [(d, d ^ bits) for d in range(8)])

    count = lax.axis_size("energy")
    near_pairs, far_pairs = [], []
    for d in range(8):
        for e in range(count):
            for pairs, target, step in (
                (near_pairs, d ^ 1, 1 if d % 2 else -1),
                (far_pairs, d, -1 if d % 2 else 1),
            ):
                if 0 <= e + step < count:
                    pairs.append((d * count + e, target * count + e + step))

    mine, pair = lesser[k, sl, c], lesser[k, 1 - sl, c]
    odd = [d for d in range(8) if d & 2]
    upper = [(s * 8 + d, (1 - s) * 8 + d) for s in range(2) for d in odd]
    lower = [(s * 8 + (d ^ 2), (1 - s) * 8 + d) for s in range(2) for d in odd]
    rim = lesser[k, 1 - b, c]
    top = lax.ppermute(rim[: NO // 2], ("slab", "freq"), upper)
    packed, part = prepare(occupations, offsets, coupling)
    last, part = lax.optimization_barrier((rim[NO // 2 :], part))
    bottom = lax.ppermute(last, ("slab", "freq"), lower)
    half = flip(part, 4)
    mixed = mix(intersection, mine, pair, top, bottom)
    mixed, packed = lax.optimization_barrier((mixed, packed))
    near = lax.ppermute(mixed, ("freq", "energy"), near_pairs)
    far = lax.ppermute(mixed, ("freq", "energy"), far_pairs)
    c1, c3 = flip(packed, 2), flip(packed, 6)
    other = lax.ppermute(half, "energy", [(e, e ^ 4) for e in range(count)])
    near, mixed, other = lax.optimization_barrier((near, mixed, other))
    own, shared = flip(mixed, 1), flip(near, 1)
    own, shared, far, packed, half, other = lax.optimization_barrier(
        (own, shared, far, packed, half, other)
    )
    swapped = [flip(x, 1) for x in (packed, c1, c3, half, other)]

    first, green = sandwich_first([own, near, shared, far], [packed, c1, c3, half, other])
    pieces = sandwich_last(green, first, swapped, retarded)
    return collect(lax.all_to_all(pieces, "freq", 0, 0))


def solution(mesh):
    return jax.shard_map(
        shards,
        mesh=mesh,
        in_specs=(
            P("energy", "slab", None, None, None),
            P("energy", "slab", None, None, None),
            P("freq", None, None),
            P("freq"),
            P("freq"),
            P("slab"),
        ),
        out_specs=P("energy", "slab", None, "freq", None),
        check_vma=False,
    )
```

```python
import functools
import jax
import jax.numpy as jnp
from jax import lax
from jax.experimental import pallas as pl
from jax.experimental.pallas import tpu as pltpu
from jax.sharding import PartitionSpec as P

NO = 512
ROWS = 64
TAIL = 16
UPPER = 384
F32 = jnp.float32
BF16 = jnp.bfloat16
MIB = 1 << 20
HBM = pl.BlockSpec(memory_space=pltpu.HBM)
SMEM = pl.BlockSpec(memory_space=pltpu.SMEM)
VMEM = pl.BlockSpec(memory_space=pltpu.VMEM)
PARAMS = pltpu.CompilerParams(vmem_limit_bytes=24 * MIB)


def shape(dims, kind):
    return jax.ShapeDtypeStruct(dims, kind)


def mul(a, b):
    return jnp.dot(a, b, preferred_element_type=F32)


def mul_t(a, b):
    return lax.dot_general(a, b, (((1,), (1,)), ((), ())), preferred_element_type=F32)


def place():
    device, b = lax.axis_index("freq"), lax.axis_index("slab")
    y, k = device >> 1, device & 1
    return y, k, (y & 1) ^ b, b, y >> 1, (lax.axis_index("energy") >> 2) & 1


def prepare_kernel(occupations, offsets, coupling, packed, half, blocks, sem):
    x = place()[5]
    copies = [
        pltpu.make_async_copy(coupling.at[t], blocks.at[t, pl.ds(0, NO)], sem.at[t])
        for t in range(2)
    ]
    for copy in copies:
        copy.start()
    row = lax.broadcasted_iota(jnp.int32, (TAIL, NO), 0)
    for t in range(2):
        whole = jnp.full((TAIL, NO), occupations[t], F32)
        high = whole.astype(BF16).astype(F32)
        middle = (whole - high).astype(BF16).astype(F32)
        low = whole - high - middle
        steps = jnp.full((TAIL, NO), offsets[t], jnp.int32).astype(F32)
        rows = jnp.where(row == 2, low, steps)
        rows = jnp.where(row == 0, high, jnp.where(row == 1, middle, rows))
        blocks[t, NO:] = rows.astype(BF16)
    for copy in copies:
        copy.wait()
    copies = [
        pltpu.make_async_copy(blocks.at[x], half, sem.at[2]),
        pltpu.make_async_copy(blocks, packed, sem.at[3]),
    ]
    for copy in copies:
        copy.start()
    for copy in copies:
        copy.wait()


def prepare(occupations, offsets, coupling):
    block = (NO + TAIL, NO)
    return pl.pallas_call(
        prepare_kernel,
        out_shape=[shape((2, *block), BF16), shape(block, BF16)],
        in_specs=[SMEM] * 2 + [HBM],
        out_specs=[HBM] * 2,
        scratch_shapes=[pltpu.VMEM((2, *block), BF16), pltpu.SemaphoreType.DMA((4,))],
        compiler_params=pltpu.CompilerParams(vmem_limit_bytes=60 * MIB),
        name="prepare",
    )(occupations, offsets, coupling)


def mix_kernel(weight, mine, pair, top, bottom, out):
    scale = weight[place()[2]]
    for cross, rows in ((top, pl.ds(0, UPPER)), (bottom, pl.ds(UPPER, NO - UPPER))):
        beside = pair[rows].astype(F32) + cross[...].astype(F32)
        out[rows] = (mine[rows].astype(F32) + scale * beside).astype(BF16)


def mix(weight, mine, pair, top, bottom):
    return pl.pallas_call(
        mix_kernel,
        out_shape=shape((NO, NO), BF16),
        in_specs=[SMEM] + [VMEM] * 4,
        out_specs=VMEM,
        compiler_params=PARAMS,
        name="mix",
    )(weight, mine, pair, top, bottom)


def add_terms(k, green, todo):
    def numbers_of(block):
        tail = block[NO:, :].astype(F32)
        scale = tail[0:1] + tail[1:2] + tail[2:3]
        return scale, (jnp.max(tail[3:4, 0:128]) > 1.5).astype(jnp.int32)

    back = k.astype(F32)
    numbers = numbers_of(todo[0])
    for n, block in enumerate(todo):
        scale, far = numbers
        if n + 1 < len(todo):
            numbers = numbers_of(todo[n + 1])
        mixture = (
            (scale + (1.0 - back)) * green[2 * far].astype(F32)
            + (scale + back) * green[2 * far + 1].astype(F32)
        ).astype(BF16)
        weights = block[:NO, :]
        left = mul(weights, mixture).astype(BF16)
        yield mul_t(left, weights)


def blocks_of(refs):
    todo = []
    for ref in refs:
        todo += [ref.at[t] for t in range(2)] if len(ref.shape) == 3 else [ref]
    return todo


def first_kernel(own, near, shared, far, home, c1, c3, half, other, out, green, gsem):
    copies = [
        pltpu.make_async_copy(src, green.at[n], gsem.at[n])
        for n, src in enumerate((own, near, shared, far))
    ]
    for copy in copies:
        copy.start()
    for copy in copies:
        copy.wait()
    todo = blocks_of((home, c1, c3, half, other))
    for n, term in enumerate(add_terms(place()[1], green, todo)):
        out[...] = term if n == 0 else out[...] + term


def last_kernel(
    green, start, s0, s1, s3, half, other, retarded, out, whole, acc, rsem
):
    _, k, sl, _, c, _ = place()
    copy = pltpu.make_async_copy(retarded.at[k, sl], whole, rsem.at[0])
    copy.start()
    todo = blocks_of((s0, s1, s3, half, other))
    for n, term in enumerate(add_terms(k, green, todo)):
        acc[...] = (start if n == 0 else acc)[...] + term
    combined = acc[...].astype(BF16)
    copy.wait()
    a, b = whole[0], whole[1]
    a_side = mul_t(combined, a).astype(BF16)
    b_side = mul_t(combined, b).astype(BF16)
    real = mul(a, a_side) + mul(b, b_side)
    imag = mul(b, a_side) - mul(a, b_side)
    first = jnp.where(c == 0, real, -imag).astype(BF16)
    second = jnp.where(c == 0, imag, real).astype(BF16)
    for dest in range(8):
        rows = slice(dest * ROWS, (dest + 1) * ROWS)
        out[dest, 0] = first[rows]
        out[dest, 1] = second[rows]


def cost(count):
    return pl.CostEstimate(
        flops=count * 4 * NO**3, bytes_accessed=(count + 10) * NO * NO * 2, transcendentals=0
    )


def sandwich_first(greens, arrays):
    return pl.pallas_call(
        first_kernel,
        out_shape=[shape((NO, NO), F32), shape((4, NO, NO), BF16)],
        in_specs=[VMEM] * 9,
        out_specs=[VMEM] * 2,
        scratch_shapes=[pltpu.SemaphoreType.DMA((4,))],
        compiler_params=PARAMS,
        cost_estimate=cost(8),
        name="sandwich_first",
    )(*greens, *arrays)


def sandwich_last(green, start, arrays, retarded):
    return pl.pallas_call(
        last_kernel,
        out_shape=shape((8, 2, ROWS, NO), BF16),
        in_specs=[VMEM] * 7 + [HBM],
        out_specs=VMEM,
        scratch_shapes=[
            pltpu.VMEM((2, NO, NO), BF16),
            pltpu.VMEM((NO, NO), F32),
            pltpu.SemaphoreType.DMA((1,)),
        ],
        compiler_params=PARAMS,
        cost_estimate=cost(11),
        name="sandwich_last",
    )(green, start, *arrays, retarded)


def collect_kernel(pieces, out, total, sem):
    b = place()[3]
    copies = []
    for n in range(4):
        k, parity = n % 2, n // 2
        total[n] = pieces[n].astype(F32) + pieces[n + 4].astype(F32)
        copies.append(pltpu.make_async_copy(total.at[n], out.at[k, parity ^ b], sem.at[n]))
        copies[-1].start()
    for copy in copies:
        copy.wait()


def collect(pieces):
    return pl.pallas_call(
        collect_kernel,
        out_shape=shape((2, 2, 2, ROWS, NO), F32),
        in_specs=[VMEM],
        out_specs=HBM,
        scratch_shapes=[pltpu.VMEM((4, 2, ROWS, NO), F32), pltpu.SemaphoreType.DMA((4,))],
        compiler_params=PARAMS,
        name="collect",
    )(pieces)


def shards(lesser, retarded, coupling, occupations, offsets, intersection):
    _, k, sl, b, c, _ = place()

    def flip(x, bits):
        return lax.ppermute(x, "freq", [(d, d ^ bits) for d in range(8)])

    count = lax.axis_size("energy")
    near_pairs, far_pairs = [], []
    for d in range(8):
        for e in range(count):
            for pairs, target, step in (
                (near_pairs, d ^ 1, 1 if d % 2 else -1),
                (far_pairs, d, -1 if d % 2 else 1),
            ):
                if 0 <= e + step < count:
                    pairs.append((d * count + e, target * count + e + step))

    mine, pair = lesser[k, sl, c], lesser[k, 1 - sl, c]
    odd = [d for d in range(8) if d & 2]
    upper = [(s * 8 + d, (1 - s) * 8 + d) for s in range(2) for d in odd]
    lower = [(s * 8 + (d ^ 2), (1 - s) * 8 + d) for s in range(2) for d in odd]
    rim = lesser[k, 1 - b, c]
    top = lax.ppermute(rim[:UPPER], ("slab", "freq"), upper)
    bottom = lax.ppermute(rim[UPPER:], ("slab", "freq"), lower)
    packed, part = prepare(occupations, offsets, coupling)
    half = flip(part, 4)
    mixed = mix(intersection, mine, pair, top, bottom)
    mixed, packed = lax.optimization_barrier((mixed, packed))
    near = lax.ppermute(mixed, ("freq", "energy"), near_pairs)
    far = lax.ppermute(mixed, ("freq", "energy"), far_pairs)
    c1, c3 = flip(packed, 2), flip(packed, 6)
    near, mixed = lax.optimization_barrier((near, mixed))
    own, shared = flip(mixed, 1), flip(near, 1)
    other = lax.ppermute(half, "energy", [(e, e ^ 4) for e in range(count)])
    own, shared, far, packed, half, other = lax.optimization_barrier(
        (own, shared, far, packed, half, other)
    )
    swapped = [flip(x, 1) for x in (packed, c1, c3, half, other)]

    first, green = sandwich_first([own, near, shared, far], [packed, c1, c3, half, other])
    pieces = sandwich_last(green, first, swapped, retarded)
    return collect(lax.all_to_all(pieces, "freq", 0, 0))


def solution(mesh):
    return jax.shard_map(
        shards,
        mesh=mesh,
        in_specs=(
            P("energy", "slab", None, None, None),
            P("energy", "slab", None, None, None),
            P("freq", None, None),
            P("freq"),
            P("freq"),
            P("slab"),
        ),
        out_specs=P("energy", "slab", None, "freq", None),
        check_vma=False,
    )
```
